512 devices in a mesh: seq: 128 (over x_hi, z, y), ch: 4 (over x_lo, core).
Axes of the slice: x: 4 (x_hi: 2, x_lo: 2; x = x_hi * 2 + x_lo), y: 8, z: 8, core: 2. Of those that a mesh axis runs over, the one named last changes fastest.
Arguments:
- values: bfloat16 [1048576, 512], P('seq', 'ch'), may hold values from -6 to 6
- factor_low: bfloat16 [64, 64], replicated, may hold values from -0.75 to 0.75
- twist_low: float32 [128, 64], replicated, may hold values from 0.25 to 1.75
- factor_mid: bfloat16 [128, 128], replicated, may hold values from -0.5 to 0.5
- twist_top: float32 [128, 128], replicated, may hold values from 0.25 to 1.75
- factor_top: bfloat16 [128, 128], replicated, may hold values from -0.5 to 0.5
- kernel_top: float32 [128, 512], P(None, 'ch'), may hold values from 0.3 to 3
- kernel_low: bfloat16 [8192, 512], P('seq', 'ch'), may hold values from -6 to 6
- inverse_top: bfloat16 [128, 128], replicated, may hold values from -0.5 to 0.5
- untwist_top: float32 [128, 128], replicated, may hold values from 0.25 to 1.75
- inverse_mid: bfloat16 [128, 128], replicated, may hold values from -0.5 to 0.5
- untwist_low: float32 [128, 64], replicated, may hold values from 0.25 to 1.75
- inverse_low: bfloat16 [64, 64], replicated, may hold values from -0.75 to 0.75
- out_weight: bfloat16 [512, 512], P('ch'), may hold values from -0.25 to 0.25
Outputs:
- layer_out: bfloat16 [1048576, 512], P(('seq', 'ch'))
The draws below stay inside these ranges and needn't reach their ends.
All inputs are finite; a program needn't handle non-finite values.
Results may differ from the reference program's by a relative error of at most 0.023.
Values may be sent and summed in bfloat16 or wider, within the bound.
No kernel may reach another device: no remote copies, remote signals or barrier semaphores. Data moves between devices by JAX's collectives and lax.ppermute only.
A program may use at most 64 MiB of HBM per device.

```python
import math
import jax
import jax.numpy as jnp
from jax import lax

TOP_DIGIT = 128
MID_DIGIT = 128
LOW_DIGIT = 64
CHANNELS = 512
LENGTH = 1048576


def level_of(own_key, shape, split, smallest, largest):
    level = 1.0
    for dim, blocks in split:
        steps = jax.random.uniform(jax.random.fold_in(jax.random.fold_in(own_key, 6), dim), (blocks,), jnp.float32, smallest / len(split), largest / len(split))
        level = level * jnp.repeat(jnp.exp(steps), shape[dim] // blocks).reshape((-1,) + (1,) * (len(shape) - 1 - dim))
    return level


def scatter_about(own_key, extent, deviation, bound, shards=(), dtype=jnp.bfloat16):
    array = deviation * jax.random.normal(own_key, extent, jnp.float32)
    if shards:
        array = array * level_of(own_key, extent, shards, -0.22, 0.18)
    return jnp.clip(array, -bound, bound).astype(dtype)


def setup_inputs(seed: int = 0) -> dict:
    splits = jax.random.split(jax.random.key(seed), 15)
    return {
        "values": scatter_about(splits[0], (LENGTH, CHANNELS), 1.0, 6.0, ((0, 128), (1, 4))),
        "factor_low": scatter_about(splits[1], (LOW_DIGIT, LOW_DIGIT), LOW_DIGIT ** -0.5, 0.75),
        "twist_low": jnp.clip(1.0 + 0.15 * jax.random.normal(splits[2], (MID_DIGIT, LOW_DIGIT), jnp.float32), 0.25, 1.75),
        "factor_mid": scatter_about(splits[3], (MID_DIGIT, MID_DIGIT), MID_DIGIT ** -0.5, 0.5),
        "twist_top": jnp.clip(1.0 + 0.15 * jax.random.normal(splits[4], (TOP_DIGIT, MID_DIGIT), jnp.float32), 0.25, 1.75),
        "factor_top": scatter_about(splits[5], (TOP_DIGIT, TOP_DIGIT), TOP_DIGIT ** -0.5, 0.5),
        "kernel_top": jnp.clip(jnp.exp(math.log(3.0) - 2.3025851 * jax.random.uniform(splits[6], (TOP_DIGIT, CHANNELS), jnp.float32) ** level_of(splits[6], (TOP_DIGIT, CHANNELS), ((1, 4),), -0.2, 0.2)), 0.3, 3.0),
        "kernel_low": scatter_about(splits[7], (MID_DIGIT * LOW_DIGIT, CHANNELS), 1.0, 6.0, ((0, 128), (1, 4))),
        "inverse_top": scatter_about(splits[8], (TOP_DIGIT, TOP_DIGIT), TOP_DIGIT ** -0.5, 0.5),
        "untwist_top": jnp.clip(1.0 + 0.15 * jax.random.normal(splits[9], (TOP_DIGIT, MID_DIGIT), jnp.float32), 0.25, 1.75),
        "inverse_mid": scatter_about(splits[10], (MID_DIGIT, MID_DIGIT), MID_DIGIT ** -0.5, 0.5),
        "untwist_low": jnp.clip(1.0 + 0.15 * jax.random.normal(splits[11], (MID_DIGIT, LOW_DIGIT), jnp.float32), 0.25, 1.75),
        "inverse_low": scatter_about(splits[12], (LOW_DIGIT, LOW_DIGIT), LOW_DIGIT ** -0.5, 0.75),
        "out_weight": scatter_about(splits[13], (CHANNELS, CHANNELS), CHANNELS ** -0.5, 0.25, ((0, 4),)),
    }


def reference(values, factor_low, twist_low, factor_mid, twist_top, factor_top, kernel_top, kernel_low, inverse_top, untwist_top, inverse_mid, untwist_low, inverse_low, out_weight):
    width = math.gcd(CHANNELS, 32)
    blocks = CHANNELS // width
    f_low = factor_low.astype(jnp.float32)
    f_mid = factor_mid.astype(jnp.float32)
    f_top = factor_top.astype(jnp.float32)
    g_top = inverse_top.astype(jnp.float32)
    g_mid = inverse_mid.astype(jnp.float32)
    g_low = inverse_low.astype(jnp.float32)

    def mix_block(begin):
        field = lax.dynamic_slice_in_dim(values, begin, width, 1).astype(jnp.float32)
        field = field.reshape(TOP_DIGIT, MID_DIGIT, LOW_DIGIT, width)
        top_prof = lax.dynamic_slice_in_dim(kernel_top, begin, width, 1)
        low_prof = lax.dynamic_slice_in_dim(kernel_low, begin, width, 1).astype(jnp.float32)
        low_prof = low_prof.reshape(MID_DIGIT, LOW_DIGIT, width)
        first = jnp.einsum("kc,abcd->abkd", f_low, field)
        first = (twist_low[None, :, :, None] * first).astype(jnp.bfloat16).astype(jnp.float32)
        second = jnp.einsum("jb,abkd->ajkd", f_mid, first)
        second = (twist_top[:, :, None, None] * second).astype(jnp.bfloat16).astype(jnp.float32)
        spectrum = jnp.einsum("ia,ajkd->ijkd", f_top, second).astype(jnp.bfloat16).astype(jnp.float32)
        filtered = spectrum * top_prof[:, None, None, :] * low_prof[None, :, :, :]
        filtered = filtered.astype(jnp.bfloat16).astype(jnp.float32)
        back = jnp.einsum("ai,ijkd->ajkd", g_top, filtered)
        back = (untwist_top[:, :, None, None] * back).astype(jnp.bfloat16).astype(jnp.float32)
        third = jnp.einsum("bj,ajkd->abkd", g_mid, back)
        third = (untwist_low[None, :, :, None] * third).astype(jnp.bfloat16).astype(jnp.float32)
        mixed = jnp.einsum("ck,abkd->abcd", g_low, third)
        gated = (mixed * jax.nn.silu(field)).astype(jnp.bfloat16)
        return gated.reshape(LENGTH, width)

    starts = (jnp.arange(blocks) * width).astype(jnp.int32)
    gated_all = lax.map(mix_block, starts)
    stride = min(LENGTH, 8192)

    def project(begin):
        rows = lax.dynamic_slice_in_dim(gated_all, begin, stride, 1)
        rows = jnp.transpose(rows, (1, 0, 2)).reshape(stride, CHANNELS)
        return jnp.dot(rows, out_weight, preferred_element_type=jnp.float32).astype(jnp.bfloat16)

    row_starts = (jnp.arange(LENGTH // stride) * stride).astype(jnp.int32)
    result = lax.map(project, row_starts)
    return result.reshape(LENGTH, CHANNELS)
```

```python
import functools

import jax
import jax.numpy as jnp
from jax import lax
from jax.experimental import pallas as pl
from jax.experimental.pallas import tpu as pltpu
from jax.sharding import PartitionSpec as P

F32 = jnp.float32
BF16 = jnp.bfloat16
STEP = 512


def iota(shape, axis):
    return lax.broadcasted_iota(jnp.int32, shape, axis)


def dot(left, right):
    return jnp.dot(left, right, preferred_element_type=F32)


def widen(source, target):
    rows = target.shape[0]

    def body(n, _):
        at = pl.multiple_of(n * STEP, STEP)
        target[pl.ds(at, STEP), :] = source[pl.ds(at, STEP), :].astype(F32)
        return 0

    lax.fori_loop(0, rows // STEP, body, 0)


def narrow(source, target):
    rows = target.shape[0]

    def body(n, _):
        at = pl.multiple_of(n * STEP, STEP)
        target[pl.ds(at, STEP), :] = source[pl.ds(at, STEP), :].astype(BF16)
        return 0

    lax.fori_loop(0, rows // STEP, body, 0)


def repeat_lanes(matrix, times):
    n = matrix.shape[1]
    shape = (n, n * times)
    pick = (lax.rem(iota(shape, 1), n) == iota(shape, 0)).astype(F32).astype(BF16)
    return dot(matrix, pick)


def column_of_row(row):
    n = row.shape[1]
    square = jnp.broadcast_to(row, (n, n))
    return jnp.sum(jnp.where(iota((n, n), 0) == iota((n, n), 1), square, 0.0), axis=1, keepdims=True)


def forward_kernel(low, values, factor_low, twist_low, factor_mid, twist_top, second, rows_f, rows_g, diag):
    mid = factor_mid.shape[0]
    times = 256 // low
    place = lax.axis_index("seq")
    tiled = repeat_lanes(factor_low[...], times)
    for t in range(times):
        block = jnp.where(iota(tiled.shape, 1) // low == t, tiled, 0.0)
        diag[t * low:(t + 1) * low, :] = block.astype(BF16)

    def lows(n, _):
        at = pl.multiple_of(n * 512, 512)
        top = values[pl.ds(at, 256), :]
        bottom = values[pl.ds(at + 256, 256), :]
        both = dot(diag[...], jnp.concatenate([top, bottom], axis=1))
        rows_f[pl.ds(at, 256), :] = both[:, :128]
        rows_f[pl.ds(at + 256, 256), :] = both[:, 128:]
        return 0

    lax.fori_loop(0, mid * low // 512, lows, 0)
    scaled = column_of_row(twist_top[pl.ds(place, 1), :]) * factor_mid[...].astype(F32)
    for k in range(low):
        matrix = (scaled * twist_low[k:k + 1, :]).astype(BF16)
        piece = rows_f[pl.ds(k, mid, stride=low), :].astype(BF16)
        rows_g[pl.ds(k, mid, stride=low), :] = dot(matrix, piece)
    narrow(rows_g, second)


def filter_kernel(low, columns, factor_top, kernel_top, kernel_low, inverse_top, untwist_top, back, rows_f, rows_g):
    top = factor_top.shape[0]
    place = lax.axis_index("seq")
    widen(columns, rows_f)
    picked = jnp.where(iota((top, top), 1) == place, untwist_top[...], 0.0)
    scale = jnp.broadcast_to(jnp.sum(picked, axis=1, keepdims=True), (top, 128))
    scale = jnp.concatenate([scale, scale], axis=1)
    profile = kernel_top[...]
    for k in range(0, low, 2):
        one = rows_f[pl.ds(k, top, stride=low), :].astype(BF16)
        two = rows_f[pl.ds(k + 1, top, stride=low), :].astype(BF16)
        spectrum = dot(factor_top[...], jnp.concatenate([one, two], axis=1)).astype(BF16).astype(F32)
        first = spectrum[:, :128] * profile * kernel_low[k:k + 1, :].astype(F32)
        other = spectrum[:, 128:] * profile * kernel_low[k + 1:k + 2, :].astype(F32)
        filtered = jnp.concatenate([first.astype(BF16), other.astype(BF16)], axis=1)
        result = scale * dot(inverse_top[...], filtered)
        rows_g[pl.ds(k, top, stride=low), :] = result[:, :128]
        rows_g[pl.ds(k + 1, top, stride=low), :] = result[:, 128:]
    narrow(rows_g, back)


def gate_block(low, third, values, inverse_low, untwist_low, start, groups, gated):
    times = 256 // low
    tiled = repeat_lanes(inverse_low[...], times)
    lane = iota(tiled.shape, 1) // low

    def body(n, _):
        at = pl.multiple_of(start + n * 256, 256)
        weights = tiled * untwist_low[pl.ds(at // 256, 1), :]
        diag = jnp.concatenate([jnp.where(lane == t, weights, 0.0).astype(BF16) for t in range(times)], axis=0)
        mixed = dot(diag, third[pl.ds(at, 256), :].astype(BF16))
        value = values[pl.ds(at, 256), :].astype(F32)
        silu = (0.5 * value) * (1.0 + jnp.tanh(0.5 * value))
        gated[pl.ds(pl.multiple_of(n * 256, 256), 256), :] = (mixed * silu).astype(BF16)
        return 0

    lax.fori_loop(0, groups, body, 0)


def third_kernel(low, turn, restored, values, inverse_mid, inverse_low, untwist_low, third, gated, rows_f, rows_g):
    mid = inverse_mid.shape[0]
    widen(restored, rows_f)
    for k in range(0, low, 2):
        one = rows_f[pl.ds(k, mid, stride=low), :].astype(BF16)
        two = rows_f[pl.ds(k + 1, mid, stride=low), :].astype(BF16)
        result = dot(inverse_mid[...], jnp.concatenate([one, two], axis=1))
        rows_g[pl.ds(k, mid, stride=low), :] = result[:, :128]
        rows_g[pl.ds(k + 1, mid, stride=low), :] = result[:, 128:]
    share = gated.shape[0]
    start = (lax.axis_index("ch") ^ turn) * share
    gate_block(low, rows_g, values, inverse_low, untwist_low, start, share // 256, gated)
    narrow(rows_g, third)


def gate_kernel(low, turns, third, values, inverse_low, untwist_low, *gated):
    for turn, target in zip(turns, gated):
        share = target.shape[0]
        start = (lax.axis_index("ch") ^ turn) * share
        gate_block(low, third, values, inverse_low, untwist_low, start, share // 256, target)


def project_kernel(*refs):
    count = (len(refs) - 1) // 2
    pieces, weights, out = refs[:count], refs[count:2 * count], refs[-1]

    def body(n, _):
        at = pl.multiple_of(n * 256, 256)
        total = dot(pieces[0][pl.ds(at, 256), :], weights[0][...])
        for piece, weight in zip(pieces[1:], weights[1:]):
            total += dot(piece[pl.ds(at, 256), :], weight[...])
        out[pl.ds(at, 256), :] = total.astype(out.dtype)
        return 0

    lax.fori_loop(0, out.shape[0] // 256, body, 0)


def call(kernel, name, out_shape, scratch, flops, *args):
    vmem = pl.BlockSpec(memory_space=pltpu.VMEM)
    outs = jax.tree.leaves(out_shape)
    moved = sum(a.size * a.dtype.itemsize for a in args) + sum(o.size * o.dtype.itemsize for o in outs)
    return pl.pallas_call(
        kernel,
        name=name,
        out_shape=out_shape,
        in_specs=[vmem] * len(args),
        out_specs=jax.tree.map(lambda _: vmem, out_shape),
        scratch_shapes=scratch,
        compiler_params=pltpu.CompilerParams(vmem_limit_bytes=40 << 20),
        cost_estimate=pl.CostEstimate(flops=flops, bytes_accessed=moved, transcendentals=0),
    )(*args)


def local(
    values,
    factor_low,
    twist_low,
    factor_mid,
    twist_top,
    factor_top,
    kernel_top,
    kernel_low,
    inverse_top,
    untwist_top,
    inverse_mid,
    untwist_low,
    inverse_low,
    out_weight,
):
    low = factor_low.shape[0]
    mid = factor_mid.shape[0]
    top = factor_top.shape[0]
    rows, width = values.shape
    ch_count = lax.axis_size("ch")
    share = rows // ch_count
    wide = pltpu.VMEM((rows, width), F32)
    shape = jax.ShapeDtypeStruct((rows, width), BF16)
    part = jax.ShapeDtypeStruct((share, width), BF16)
    unit = 2 * rows * width

    def swap(array, turn):
        return lax.ppermute(array, "ch", [(c, c ^ turn) for c in range(ch_count)])

    second = call(
        functools.partial(forward_kernel, low), "forward", shape,
        [wide, wide, pltpu.VMEM((256, 256), BF16)], unit * (low + mid),
        values, factor_low, twist_low.T, factor_mid, twist_top,
    )
    columns = lax.all_to_all(second.reshape(mid, low, width), "seq", 0, 0, tiled=True)
    weights = [out_weight] + [swap(out_weight, turn) for turn in range(1, ch_count)]
    back = call(
        functools.partial(filter_kernel, low), "filter", shape, [wide, wide], unit * 2 * top,
        columns.reshape(rows, width), factor_top, kernel_top, kernel_low, inverse_top, untwist_top,
    )
    restored = lax.all_to_all(back.reshape(top, low, width), "seq", 0, 0, tiled=True)
    scale = untwist_low.reshape(-1, 256)
    third, far = call(
        functools.partial(third_kernel, low, 2), "third", (shape, part), [wide, wide],
        unit * (mid + low // 4), restored.reshape(rows, width), values, inverse_mid, inverse_low, scale,
    )
    far = swap(far, 2)
    across, = call(
        functools.partial(gate_kernel, low, (3,)), "gate", (part,), [], unit * low // 4,
        third, values, inverse_low, scale,
    )
    across = swap(across, 3)
    near, own = call(
        functools.partial(gate_kernel, low, (1, 0)), "gate", (part, part), [], unit * low // 2,
        third, values, inverse_low, scale,
    )
    near = swap(near, 1)
    return call(
        project_kernel, "project", jax.ShapeDtypeStruct((share, out_weight.shape[1]), BF16), [],
        2 * share * out_weight.shape[1] ** 2,
        own, near, far, across, *weights,
    )


def solution(mesh):
    return jax.shard_map(
        local,
        mesh=mesh,
        in_specs=(
            P("seq", "ch"),
            P(),
            P(),
            P(),
            P(),
            P(),
            P(None, "ch"),
            P("seq", "ch"),
            P(),
            P(),
            P(),
            P(),
            P(),
            P("ch", None),
        ),
        out_specs=P(("seq", "ch"), None),
        check_vma=False,
    )
```

```python
import functools

import jax
import jax.numpy as jnp
from jax import lax
from jax.experimental import pallas as pl
from jax.experimental.pallas import tpu as pltpu
from jax.sharding import PartitionSpec as P

F32 = jnp.float32
BF16 = jnp.bfloat16
LANES = 128
HALF = 64
PITCH = 72


def iota(shape, axis):
    return lax.broadcasted_iota(jnp.int32, shape, axis)


def dot(left, right):
    return jnp.dot(left, right, preferred_element_type=F32)


def repeat_lanes(matrix, times):
    n = matrix.shape[1]
    shape = (n, n * times)
    pick = (lax.rem(iota(shape, 1), n) == iota(shape, 0)).astype(F32).astype(BF16)
    return dot(matrix, pick)


def column_of_row(row):
    n = row.shape[1]
    square = jnp.broadcast_to(row, (n, n))
    return jnp.sum(jnp.where(iota((n, n), 0) == iota((n, n), 1), square, 0.0), axis=1, keepdims=True)


def trade_halves(one, two):
    low = iota(one.shape, 1) < HALF
    return jnp.where(low, one, pltpu.roll(two, HALF, 1)), jnp.where(low, pltpu.roll(one, HALF, 1), two)


def forward_kernel(low, values, factor_low, twist_low, factor_mid, twist_top, kernel_low, message, rows_f, diag):
    mid = factor_mid.shape[0]
    times = 256 // low
    place = lax.axis_index("seq")
    tiled = repeat_lanes(factor_low[...], times)
    for t in range(times):
        block = jnp.where(iota(tiled.shape, 1) // low == t, tiled, 0.0)
        diag[t * low:(t + 1) * low, :] = block.astype(BF16)

    def lows(n, _):
        at = pl.multiple_of(n * 512, 512)
        top = values[pl.ds(at, 256), :]
        bottom = values[pl.ds(at + 256, 256), :]
        both = dot(diag[...], jnp.concatenate([top, bottom], axis=1))
        for t in range(2 * times):
            to = pl.multiple_of((n * 2 * times + t) * PITCH, 8)
            side = t // times * LANES
            at = t % times * low
            rows_f[pl.ds(to, low), :] = both[at:at + low, side:side + LANES]
        return 0

    lax.fori_loop(0, mid * low // 512, lows, 0)
    scaled = column_of_row(twist_top[pl.ds(place, 1), :]) * factor_mid[...].astype(F32)
    profile = kernel_low[...].astype(F32)
    turned = pltpu.roll(profile, HALF, 1)
    for k in range(low):
        matrix = (scaled * twist_low[k:k + 1, :]).astype(BF16)
        second = dot(matrix, rows_f[pl.ds(k, mid, stride=PITCH), :].astype(BF16))
        halves = trade_halves(second[:HALF], second[HALF:])
        for h, (half, row) in enumerate(zip(halves, (profile, turned))):
            to = (2 * k + h) * PITCH
            message[to:to + HALF, :] = half.astype(BF16)
            message[to + HALF:to + PITCH, :] = jnp.broadcast_to(row[k:k + 1, :], (PITCH - HALF, LANES)).astype(BF16)


def middle_kernel(columns, factor_top, kernel_top, inverse_top, untwist_top, inverse_mid, untwist_low, third,
                  rows_f, rows_g, profile):
    top = factor_top.shape[0]

    def widen(n, _):
        at = pl.multiple_of(n * 8 * PITCH, 8 * PITCH)
        rows_f[pl.ds(at, 8 * PITCH), :] = columns[pl.ds(at, 8 * PITCH), :].astype(F32)
        return 0

    lax.fori_loop(0, top // 8, widen, 0)
    rows = rows_f[pl.ds(HALF, 2 * HALF, stride=PITCH), :]
    profile[...] = trade_halves(rows[:HALF], rows[HALF:])[0]
    for r in range(0, HALF, 2):
        one = rows_f[pl.ds(r, top, stride=PITCH), :].astype(BF16)
        two = rows_f[pl.ds(r + 1, top, stride=PITCH), :].astype(BF16)
        spectrum = dot(factor_top[...], jnp.concatenate([one, two], axis=1)).astype(BF16).astype(F32)
        first = spectrum[:, :LANES] * kernel_top[...] * profile[r:r + 1, :]
        other = spectrum[:, LANES:] * kernel_top[...] * profile[r + 1:r + 2, :]
        filtered = jnp.concatenate([first.astype(BF16), other.astype(BF16)], axis=1)
        back = dot(inverse_top[...], filtered)
        rows_g[pl.ds(r, top, stride=PITCH), :] = back[:, :LANES] * untwist_top[r * top:(r + 1) * top, :]
        rows_g[pl.ds(r + 1, top, stride=PITCH), :] = back[:, LANES:] * untwist_top[(r + 1) * top:(r + 2) * top, :]

    def inverse(n, _):
        sides = []
        for m in range(2):
            at = pl.multiple_of((n * 4 + m * 2) * PITCH, 8)
            upper, lower = trade_halves(rows_g[pl.ds(at, HALF), :], rows_g[pl.ds(at + PITCH, HALF), :])
            sides.append(jnp.concatenate([upper.astype(BF16), lower.astype(BF16)], axis=0))
        result = dot(inverse_mid[...], jnp.concatenate(sides, axis=1))
        for m in range(2):
            side = result[:, m * LANES:(m + 1) * LANES] * untwist_low[...]
            for q in range(4):
                pair = trade_halves(side[q * 32:q * 32 + 16], side[q * 32 + 16:q * 32 + 32])
                for p in range(2):
                    to = pl.multiple_of((n * 4 + m * 2 + p) * HALF + q * 16, 16)
                    third[pl.ds(to, 16), :] = pair[p].astype(BF16)
        return 0

    lax.fori_loop(0, top // 4, inverse, 0)


def prepare_kernel(kernel_top, untwist_top, untwist_low, *refs):
    sources, targets, (profile, scale_top, scale_low) = refs[:4], refs[4:8], refs[8:]
    place = lax.axis_index("seq")
    top = untwist_top.shape[0]
    shape = (top, LANES)
    lower = iota(shape, 1) < HALF
    whole = kernel_top[...]
    turned = pltpu.roll(whole, HALF, 1)
    first = lax.rem(place, 2) == 0
    profile[...] = jnp.where(first, jnp.where(lower, whole, turned), jnp.where(lower, turned, whole))
    scale_low[...] = jnp.broadcast_to(column_of_row(untwist_low[pl.ds(place // 2, 1), :]), scale_low.shape)
    for r in range(HALF):
        one = jnp.broadcast_to(untwist_top[:, r:r + 1], shape)
        two = jnp.broadcast_to(untwist_top[:, HALF + r:HALF + r + 1], shape)
        scale_top[r * top:(r + 1) * top, :] = jnp.where(lower, one, two)
    for source, target in zip(sources, targets):
        def body(n, _):
            at = pl.multiple_of(n * 256, 256)
            value = source[pl.ds(at, 256), :].astype(F32)
            target[pl.ds(at, 256), :] = (0.5 * value) * (1.0 + jnp.tanh(0.5 * value))
            return 0

        lax.fori_loop(0, source.shape[0] // 256, body, 0)


def last_kernel(low, third, inverse_low, *refs):
    silus, weights, out, rows_f, gated, result, sem = refs[:4], refs[4:8], refs[8], refs[9], refs[10], refs[11], refs[12]
    pitch = LANES + 8
    place = lax.axis_index("ch")

    def widen(k, _):
        for h in range(2):
            for t in range(4):
                source = pl.multiple_of(((k * 2 + h) * 4 + (place ^ t)) * 16, 16)
                to = pl.multiple_of(k * pitch + (h * 4 + t) * 16, 8)
                rows_f[pl.ds(to, 16), :] = third[pl.ds(source, 16), :].astype(F32)
        return 0

    lax.fori_loop(0, low, widen, 0)
    block = 4 * low
    copies = []
    for g in range(4):
        for b in range(4 * g, 4 * g + 4):
            for t in range(4):
                one = rows_f[pl.ds(t * 16 + b, low, stride=pitch), :]
                two = rows_f[pl.ds((4 + t) * 16 + b, low, stride=pitch), :]
                pair = trade_halves(one, two)
                mixed = dot(inverse_low[...], jnp.concatenate([p.astype(BF16) for p in pair], axis=1))
                for p in range(2):
                    at = (p * 16 + b) * low
                    gate = silus[t][at:at + low, :]
                    gated[at:at + low, t * LANES:(t + 1) * LANES] = (
                        mixed[:, p * LANES:(p + 1) * LANES] * gate
                    ).astype(BF16)
        for p in range(2):
            at = (p * 4 + g) * block
            total = dot(gated[at:at + block, :LANES], weights[0][...])
            for t in range(1, 4):
                total += dot(gated[at:at + block, t * LANES:(t + 1) * LANES], weights[t][...])
            result[at:at + block, :] = total.astype(BF16)
            slot = g * 2 + p
            copy = pltpu.make_async_copy(result.at[pl.ds(at, block)], out.at[pl.ds(at, block)], sem.at[slot])
            copy.start()
            copies.append(copy)
    for copy in copies:
        copy.wait()


def call(kernel, name, out_shape, scratch, flops, *args, limit=40 << 20, out_spec=None):
    vmem = pl.BlockSpec(memory_space=pltpu.VMEM)
    outs = jax.tree.leaves(out_shape)
    moved = sum(a.size * a.dtype.itemsize for a in args) + sum(o.size * o.dtype.itemsize for o in outs)
    return pl.pallas_call(
        kernel,
        name=name,
        out_shape=out_shape,
        in_specs=[vmem] * len(args),
        out_specs=jax.tree.map(lambda _: out_spec or vmem, out_shape),
        scratch_shapes=scratch,
        compiler_params=pltpu.CompilerParams(vmem_limit_bytes=limit),
        cost_estimate=pl.CostEstimate(flops=flops, bytes_accessed=moved, transcendentals=0),
    )(*args)


def local(
    values,
    factor_low,
    twist_low,
    factor_mid,
    twist_top,
    factor_top,
    kernel_top,
    kernel_low,
    inverse_top,
    untwist_top,
    inverse_mid,
    untwist_low,
    inverse_low,
    out_weight,
):
    low = factor_low.shape[0]
    mid = factor_mid.shape[0]
    top = factor_top.shape[0]
    rows, width = values.shape
    ch_place = lax.axis_index("ch")
    ch_count = lax.axis_size("ch")
    share = rows // ch_count
    columns_out = out_weight.shape[1]
    unit = 2 * rows * width
    padded = pltpu.VMEM((top * PITCH, width), F32)

    def swap(array, turn):
        if turn == 0:
            return array
        return lax.ppermute(array, "ch", [(c, c ^ turn) for c in range(ch_count)])

    message = call(
        functools.partial(forward_kernel, low), "forward", jax.ShapeDtypeStruct((2 * low * PITCH, width), BF16),
        [padded, pltpu.VMEM((256, 256), BF16)], unit * (low + mid),
        values, factor_low, twist_low.T, factor_mid, twist_top, kernel_low, limit=60 << 20,
    )
    columns = lax.all_to_all(message.reshape(2 * low, PITCH, width), "seq", 0, 0, tiled=True)

    turns = range(ch_count)
    shares = [
        swap(lax.dynamic_slice_in_dim(values, (ch_place ^ turn) * share, share, 0), turn) for turn in turns
    ]
    weights = [swap(out_weight, turn) for turn in turns]
    *silus, profile, scale_top, scale_low = call(
        prepare_kernel, "prepare",
        [jax.ShapeDtypeStruct((share, width), F32)] * ch_count
        + [jax.ShapeDtypeStruct((n, width), F32) for n in (top, HALF * top, mid)],
        [], unit, kernel_top, untwist_top, untwist_low.T, *shares,
    )
    columns, silus, weights, profile, scale_top, scale_low = lax.optimization_barrier(
        (columns, silus, weights, profile, scale_top, scale_low)
    )

    third = call(
        middle_kernel, "middle", jax.ShapeDtypeStruct((rows, width), BF16),
        [padded, padded, pltpu.VMEM((HALF, width), F32)], unit * (2 * top + mid),
        columns.reshape(top * PITCH, width), factor_top, profile, inverse_top, scale_top, inverse_mid, scale_low,
    )
    third = lax.all_to_all(third.reshape(top * ch_count, -1, width), ("seq", "ch"), 0, 0, tiled=True)
    return call(
        functools.partial(last_kernel, low), "last", jax.ShapeDtypeStruct((share, columns_out), BF16),
        [
            pltpu.VMEM((low * (width + 8), width), F32),
            pltpu.VMEM((share, columns_out), BF16),
            pltpu.VMEM((share, columns_out), BF16),
            pltpu.SemaphoreType.DMA((8,)),
        ],
        unit * low // 2 + 2 * share * columns_out ** 2,
        third.reshape(rows, width), inverse_low, *silus, *weights,
        out_spec=pl.BlockSpec(memory_space=pl.ANY),
    )


def solution(mesh):
    return jax.shard_map(
        local,
        mesh=mesh,
        in_specs=(
            P("seq", "ch"),
            P(),
            P(),
            P(),
            P(),
            P(),
            P(None, "ch"),
            P("seq", "ch"),
            P(),
            P(),
            P(),
            P(),
            P(),
            P("ch", None),
        ),
        out_specs=P(("seq", "ch"), None),
        check_vma=False,
    )
```

```python
import functools

import jax
import jax.numpy as jnp
from jax import lax
from jax.experimental import pallas as pl
from jax.experimental.pallas import tpu as pltpu
from jax.sharding import PartitionSpec as P

F32 = jnp.float32
BF16 = jnp.bfloat16
LANES = 128
HALF = 64
PITCH = 72


def iota(shape, axis):
    return lax.broadcasted_iota(jnp.int32, shape, axis)


def dot(left, right):
    return jnp.dot(left, right, preferred_element_type=F32)


def repeat_lanes(matrix, times):
    n = matrix.shape[1]
    shape = (n, n * times)
    pick = (lax.rem(iota(shape, 1), n) == iota(shape, 0)).astype(F32).astype(BF16)
    return dot(matrix, pick)


def column_of_row(row):
    n = row.shape[1]
    square = jnp.broadcast_to(row, (n, n))
    return jnp.sum(jnp.where(iota((n, n), 0) == iota((n, n), 1), square, 0.0), axis=1, keepdims=True)


def trade_halves(one, two):
    low = iota(one.shape, 1) < HALF
    return jnp.where(low, one, pltpu.roll(two, HALF, 1)), jnp.where(low, pltpu.roll(one, HALF, 1), two)


def forward_kernel(low, values, factor_low, twist_low, factor_mid, twist_top, kernel_low, message,
                   held, small, wide, row, twist, rows_f, diag, out, sem_in, sem_out):
    mid = factor_mid.shape[0]
    times = 256 // low
    chunk = mid * low // 4
    place = lax.axis_index("seq")
    loads = [
        pltpu.make_async_copy(values.at[pl.ds(n * chunk, chunk)], held.at[pl.ds(n * chunk, chunk)], sem_in.at[n])
        for n in range(4)
    ]
    fetch_low = pltpu.make_async_copy(factor_low, small, sem_in.at[4])
    others = [
        pltpu.make_async_copy(factor_mid, wide, sem_in.at[5]),
        pltpu.make_async_copy(twist_top.at[pl.ds(place // 8 * 8, 8)], row, sem_in.at[6]),
        pltpu.make_async_copy(twist_low, twist, sem_in.at[7]),
    ]
    fetch_low.start()
    for copy in loads + others:
        copy.start()
    fetch_low.wait()
    tiled = repeat_lanes(small[...], times)
    for t in range(times):
        block = jnp.where(iota(tiled.shape, 1) // low == t, tiled, 0.0)
        diag[t * low:(t + 1) * low, :] = block.astype(BF16)
    for n in range(mid * low // 512):
        if n % 4 == 0:
            loads[n // 4].wait()
        at = n * 512
        both = dot(diag[...], jnp.concatenate([held[at:at + 256, :], held[at + 256:at + 512, :]], axis=1))
        for t in range(2 * times):
            to = (n * 2 * times + t) * PITCH
            side = t // times * LANES
            at = t % times * low
            rows_f[to:to + low, :] = both[at:at + low, side:side + LANES]
    for copy in others:
        copy.wait()
    scaled = column_of_row(row[pl.ds(lax.rem(place, 8), 1), :]) * wide[...].astype(F32)
    profile = kernel_low[...].astype(F32)
    turned = pltpu.roll(profile, HALF, 1)
    stores = []
    for k in range(low):
        matrix = (scaled * twist[k:k + 1, :]).astype(BF16)
        second = dot(matrix, rows_f[pl.ds(k, mid, stride=PITCH), :].astype(BF16))
        halves = trade_halves(second[:HALF], second[HALF:])
        for h, (half, line) in enumerate(zip(halves, (profile, turned))):
            to = (2 * k + h) * PITCH
            out[to:to + HALF, :] = half.astype(BF16)
            out[to + HALF:to + PITCH, :] = jnp.broadcast_to(line[k:k + 1, :], (PITCH - HALF, LANES)).astype(BF16)
        if k % 16 == 15:
            size = 32 * PITCH
            at = k // 16 * size
            store = pltpu.make_async_copy(
                out.at[pl.ds(at, size)], message.at[pl.ds(at, size)], sem_out.at[k // 16]
            )
            store.start()
            stores.append(store)
    for store in stores:
        store.wait()


def middle_kernel(columns, factor_top, kernel_top, inverse_top, scale_top, inverse_mid, untwist_low, third,
                  held, out, rows_f, rows_g, whole, lines, forth, reverse, scale, across, twist, sem, sem_in, sem_out):
    top = forth.shape[0]
    place = lax.axis_index("seq")
    pairs = ((factor_top, forth), (kernel_top, whole), (inverse_top, reverse), (inverse_mid, across),
             (untwist_low.at[pl.ds(place // 16 * 8, 8)], twist))
    copies = [pltpu.make_async_copy(a, b, sem.at[n]) for n, (a, b) in enumerate(pairs)]
    quarter = HALF * top // 4
    scales = [
        pltpu.make_async_copy(
            scale_top.at[pl.ds(n * quarter, quarter)], scale.at[pl.ds(n * quarter, quarter)], sem_in.at[4 + n]
        )
        for n in range(4)
    ]
    size = top // 4 * PITCH
    loads = [
        pltpu.make_async_copy(columns.at[pl.ds(n * size, size)], held.at[pl.ds(n * size, size)], sem_in.at[n])
        for n in range(4)
    ]
    for copy in loads + copies + scales:
        copy.start()
    for n in range(top // 8):
        if n % 4 == 0:
            loads[n // 4].wait()
        at = n * 8 * PITCH
        rows_f[at:at + 8 * PITCH, :] = held[at:at + 8 * PITCH, :].astype(F32)
    rows = rows_f[pl.ds(HALF, 2 * HALF, stride=PITCH), :]
    lines[...] = trade_halves(rows[:HALF], rows[HALF:])[0]
    for copy in copies:
        copy.wait()
    lower = iota((top, LANES), 1) < HALF
    all_top = whole[...]
    turned = pltpu.roll(all_top, HALF, 1)
    keep = lower == (lax.rem(place, 2) == 0)
    whole[...] = jnp.where(keep, all_top, turned)
    scale_low = jnp.broadcast_to(column_of_row(twist[pl.ds(lax.rem(place // 2, 8), 1), :]), (across.shape[0], LANES))

    for r in range(0, HALF, 2):
        if r % 16 == 0:
            scales[r // 16].wait()
        one = rows_f[pl.ds(r, top, stride=PITCH), :].astype(BF16)
        two = rows_f[pl.ds(r + 1, top, stride=PITCH), :].astype(BF16)
        spectrum = dot(forth[...], jnp.concatenate([one, two], axis=1)).astype(BF16).astype(F32)
        first = spectrum[:, :LANES] * whole[...] * lines[r:r + 1, :]
        other = spectrum[:, LANES:] * whole[...] * lines[r + 1:r + 2, :]
        filtered = jnp.concatenate([first.astype(BF16), other.astype(BF16)], axis=1)
        back = dot(reverse[...], filtered)
        rows_g[pl.ds(r, top, stride=PITCH), :] = back[:, :LANES] * scale[r * top:(r + 1) * top, :].astype(F32)
        rows_g[pl.ds(r + 1, top, stride=PITCH), :] = back[:, LANES:] * scale[(r + 1) * top:(r + 2) * top, :].astype(F32)

    part = 32 * HALF
    stores = []
    for n in range(top // 4):
        sides = []
        for m in range(2):
            at = (n * 4 + m * 2) * PITCH
            upper, under = trade_halves(rows_g[at:at + HALF, :], rows_g[at + PITCH:at + PITCH + HALF, :])
            sides.append(jnp.concatenate([upper.astype(BF16), under.astype(BF16)], axis=0))
        result = dot(across[...], jnp.concatenate(sides, axis=1))
        for m in range(2):
            side = result[:, m * LANES:(m + 1) * LANES] * scale_low
            for q in range(4):
                pair = trade_halves(side[q * 32:q * 32 + 16], side[q * 32 + 16:q * 32 + 32])
                for p in range(2):
                    to = (n * 4 + m * 2 + p) * HALF + q * 16
                    out[to:to + 16, :] = pair[p].astype(BF16)
        if n % 8 == 7:
            at = n // 8 * part
            store = pltpu.make_async_copy(out.at[pl.ds(at, part)], third.at[pl.ds(at, part)], sem_out.at[n // 8])
            store.start()
            stores.append(store)
    for store in stores:
        store.wait()


def spread_kernel(untwist_top, scale_top):
    top = untwist_top.shape[0]
    shape = (top, LANES)
    lower = iota(shape, 1) < HALF
    for r in range(HALF):
        one = jnp.broadcast_to(untwist_top[:, r:r + 1], shape)
        two = jnp.broadcast_to(untwist_top[:, HALF + r:HALF + r + 1], shape)
        scale_top[r * top:(r + 1) * top, :] = jnp.where(lower, one, two).astype(BF16)


def silu_kernel(*refs):
    sources, target = refs[:-1], refs[-1]
    for t, source in enumerate(sources):
        def body(n, _):
            at = pl.multiple_of(n * 256, 256)
            value = source[pl.ds(at, 256), :].astype(F32)
            target[t, pl.ds(at, 256), :] = ((0.5 * value) * (1.0 + jnp.tanh(0.5 * value))).astype(BF16)
            return 0

        lax.fori_loop(0, source.shape[0] // 256, body, 0)


def last_kernel(low, third, inverse_low, silu, *refs):
    weights, out = refs[:4], refs[4]
    held, small, gates, matrix, rows_f, gated, result, sem, sem_in, sem_gate, sem_out = refs[5:]
    pitch = LANES + 8
    block = 4 * low
    place = lax.axis_index("ch")
    part = low * LANES // 4
    loads = [
        pltpu.make_async_copy(third.at[pl.ds(n * part, part)], held.at[pl.ds(n * part, part)], sem_in.at[n])
        for n in range(4)
    ]
    fetch_low = pltpu.make_async_copy(inverse_low, small, sem.at[4])
    fetch_gates = [
        pltpu.make_async_copy(
            silu.at[:, pl.ds(at, block)], gates.at[:, pl.ds(at, block)], sem_gate.at[n]
        )
        for n, at in enumerate((p * 4 + g) * block for g in range(4) for p in range(2))
    ]
    fetch_weights = [pltpu.make_async_copy(w, matrix.at[pl.ds(t * LANES, LANES)], sem.at[t]) for t, w in enumerate(weights)]
    for copy in loads + [fetch_low] + fetch_gates[:2] + fetch_weights + fetch_gates[2:]:
        copy.start()
    for n in range(4):
        loads[n].wait()
        for k in range(n * low // 4, (n + 1) * low // 4):
            for h in range(2):
                for t in range(4):
                    source = pl.multiple_of(((k * 2 + h) * 4 + (place ^ t)) * 16, 16)
                    to = k * pitch + (h * 4 + t) * 16
                    rows_f[to:to + 16, :] = held[pl.ds(source, 16), :].astype(F32)
    fetch_low.wait()
    copies = []
    for g in range(4):
        for p in range(2):
            fetch_gates[2 * g + p].wait()
        for b in range(4 * g, 4 * g + 4):
            for t in range(4):
                one = rows_f[pl.ds(t * 16 + b, low, stride=pitch), :]
                two = rows_f[pl.ds((4 + t) * 16 + b, low, stride=pitch), :]
                pair = trade_halves(one, two)
                mixed = dot(small[...], jnp.concatenate([p.astype(BF16) for p in pair], axis=1))
                for p in range(2):
                    at = (p * 16 + b) * low
                    gated[at:at + low, t * LANES:(t + 1) * LANES] = (
                        mixed[:, p * LANES:(p + 1) * LANES] * gates[t, at:at + low, :].astype(F32)
                    ).astype(BF16)
        if g == 0:
            for copy in fetch_weights:
                copy.wait()
        for p in range(2):
            at = (p * 4 + g) * block
            result[at:at + block, :] = dot(gated[at:at + block, :], matrix[...]).astype(BF16)
            copy = pltpu.make_async_copy(
                result.at[pl.ds(at, block)], out.at[pl.ds(at, block)], sem_out.at[g * 2 + p]
            )
            copy.start()
            copies.append(copy)
    for copy in copies:
        copy.wait()


def call(kernel, name, out_shape, scratch, flops, *args, limit=40 << 20, far=(), out_spec=None):
    vmem, hbm = pl.BlockSpec(memory_space=pltpu.VMEM), pl.BlockSpec(memory_space=pl.ANY)
    outs = jax.tree.leaves(out_shape)
    moved = sum(a.size * a.dtype.itemsize for a in args) + sum(o.size * o.dtype.itemsize for o in outs)
    return pl.pallas_call(
        kernel,
        name=name,
        out_shape=out_shape,
        in_specs=[hbm if n in far else vmem for n in range(len(args))],
        out_specs=jax.tree.map(lambda _: out_spec or vmem, out_shape),
        scratch_shapes=scratch,
        compiler_params=pltpu.CompilerParams(vmem_limit_bytes=limit),
        cost_estimate=pl.CostEstimate(flops=flops, bytes_accessed=moved, transcendentals=0),
    )(*args)


def local(
    values,
    factor_low,
    twist_low,
    factor_mid,
    twist_top,
    factor_top,
    kernel_top,
    kernel_low,
    inverse_top,
    untwist_top,
    inverse_mid,
    untwist_low,
    inverse_low,
    out_weight,
):
    low = factor_low.shape[0]
    mid = factor_mid.shape[0]
    top = factor_top.shape[0]
    rows, width = values.shape
    ch_place = lax.axis_index("ch")
    ch_count = lax.axis_size("ch")
    share = rows // ch_count
    columns_out = out_weight.shape[1]
    unit = 2 * rows * width
    padded = pltpu.VMEM((top * PITCH, width), F32)

    def swap(array, turn):
        if turn == 0:
            return array
        return lax.ppermute(array, "ch", [(c, c ^ turn) for c in range(ch_count)])

    message = call(
        functools.partial(forward_kernel, low), "forward", jax.ShapeDtypeStruct((2 * low * PITCH, width), BF16),
        [
            pltpu.VMEM((rows, width), BF16),
            pltpu.VMEM((low, low), BF16),
            pltpu.VMEM((mid, mid), BF16),
            pltpu.VMEM((8, mid), F32),
            pltpu.VMEM((low, mid), F32),
            padded,
            pltpu.VMEM((256, 256), BF16),
            pltpu.VMEM((2 * low * PITCH, width), BF16),
            pltpu.SemaphoreType.DMA((8,)),
            pltpu.SemaphoreType.DMA((4,)),
        ], unit * (low + mid),
        values, factor_low, twist_low.T, factor_mid, twist_top, kernel_low,
        limit=60 << 20, far=range(5), out_spec=pl.BlockSpec(memory_space=pl.ANY),
    )
    columns = lax.all_to_all(message.reshape(2 * low, PITCH, width), "seq", 0, 0, tiled=True)

    turns = range(ch_count)
    shares = [
        swap(lax.dynamic_slice_in_dim(values, (ch_place ^ turn) * share, share, 0), turn) for turn in turns
    ]
    scale_top = call(
        spread_kernel, "spread", jax.ShapeDtypeStruct((HALF * top, width), BF16), [], unit, untwist_top,
        limit=60 << 20,
    )
    columns, shares, scale_top = lax.optimization_barrier((columns, shares, scale_top))
    third = call(
        middle_kernel, "middle", jax.ShapeDtypeStruct((rows, width), BF16),
        [
            pltpu.VMEM((top * PITCH, width), BF16),
            pltpu.VMEM((rows, width), BF16),
            padded,
            padded,
            pltpu.VMEM((top, width), F32),
            pltpu.VMEM((HALF, width), F32),
            pltpu.VMEM((top, top), BF16),
            pltpu.VMEM((top, top), BF16),
            pltpu.VMEM((HALF * top, width), BF16),
            pltpu.VMEM((mid, mid), BF16),
            pltpu.VMEM((8, mid), F32),
            pltpu.SemaphoreType.DMA((5,)),
            pltpu.SemaphoreType.DMA((8,)),
            pltpu.SemaphoreType.DMA((4,)),
        ], unit * (2 * top + mid),
        columns.reshape(top * PITCH, width), factor_top, kernel_top, inverse_top, scale_top, inverse_mid,
        untwist_low.T, limit=60 << 20, far=range(7), out_spec=pl.BlockSpec(memory_space=pl.ANY),
    )
    third, shares, out_weight = lax.optimization_barrier((third, shares, out_weight))
    weights = [swap(out_weight, turn) for turn in turns]
    silu = call(
        silu_kernel, "silu", jax.ShapeDtypeStruct((ch_count, share, width), BF16), [], unit, *shares, limit=60 << 20
    )
    third = lax.all_to_all(third.reshape(top * ch_count, -1, width), ("seq", "ch"), 0, 0, tiled=True)
    return call(
        functools.partial(last_kernel, low), "last", jax.ShapeDtypeStruct((share, columns_out), BF16),
        [
            pltpu.VMEM((rows, width), BF16),
            pltpu.VMEM((low, low), BF16),
            pltpu.VMEM((ch_count, share, width), BF16),
            pltpu.VMEM((ch_count * width, columns_out), BF16),
            pltpu.VMEM((low * (width + 8), width), F32),
            pltpu.VMEM((share, columns_out), BF16),
            pltpu.VMEM((share, columns_out), BF16),
            pltpu.SemaphoreType.DMA((5,)),
            pltpu.SemaphoreType.DMA((4,)),
            pltpu.SemaphoreType.DMA((8,)),
            pltpu.SemaphoreType.DMA((8,)),
        ],
        unit * low // 2 + 2 * share * columns_out ** 2,
        third.reshape(rows, width), inverse_low, silu, *weights,
        limit=60 << 20, far=range(3 + ch_count), out_spec=pl.BlockSpec(memory_space=pl.ANY),
    )


def solution(mesh):
    return jax.shard_map(
        local,
        mesh=mesh,
        in_specs=(
            P("seq", "ch"),
            P(),
            P(),
            P(),
            P(),
            P(),
            P(None, "ch"),
            P("seq", "ch"),
            P(),
            P(),
            P(),
            P(),
            P(),
            P("ch", None),
        ),
        out_specs=P(("seq", "ch"), None),
        check_vma=False,
    )
```

```python
import functools

import jax
import jax.numpy as jnp
from jax import lax
from jax.experimental import pallas as pl
from jax.experimental.pallas import tpu as pltpu
from jax.sharding import PartitionSpec as P

F32 = jnp.float32
BF16 = jnp.bfloat16
LANES = 128
HALF = 64
PITCH = 72


def iota(shape, axis):
    return lax.broadcasted_iota(jnp.int32, shape, axis)


def dot(left, right):
    return jnp.dot(left, right, preferred_element_type=F32)


def repeat_lanes(matrix, times):
    n = matrix.shape[1]
    shape = (n, n * times)
    pick = (lax.rem(iota(shape, 1), n) == iota(shape, 0)).astype(F32).astype(BF16)
    return dot(matrix, pick)


def column_of_row(row):
    n = row.shape[1]
    square = jnp.broadcast_to(row, (n, n))
    return jnp.sum(jnp.where(iota((n, n), 0) == iota((n, n), 1), square, 0.0), axis=1, keepdims=True)


def trade_halves(one, two):
    low = iota(one.shape, 1) < HALF
    return jnp.where(low, one, pltpu.roll(two, HALF, 1)), jnp.where(low, pltpu.roll(one, HALF, 1), two)


def forward_kernel(low, values, factor_low, twist_low, factor_mid, twist_top, kernel_low, message,
                   held, small, wide, row, twist, rows_f, diag, out, sem_in, sem_out):
    mid = factor_mid.shape[0]
    times = 256 // low
    chunk = mid * low // 4
    place = lax.axis_index("seq")
    loads = [
        pltpu.make_async_copy(values.at[pl.ds(n * chunk, chunk)], held.at[pl.ds(n * chunk, chunk)], sem_in.at[n])
        for n in range(4)
    ]
    fetch_low = pltpu.make_async_copy(factor_low, small, sem_in.at[4])
    others = [
        pltpu.make_async_copy(factor_mid, wide, sem_in.at[5]),
        pltpu.make_async_copy(twist_top.at[pl.ds(place // 8 * 8, 8)], row, sem_in.at[6]),
        pltpu.make_async_copy(twist_low, twist, sem_in.at[7]),
    ]
    fetch_low.start()
    for copy in loads + others:
        copy.start()
    fetch_low.wait()
    tiled = repeat_lanes(small[...], times)
    for t in range(times):
        block = jnp.where(iota(tiled.shape, 1) // low == t, tiled, 0.0)
        diag[t * low:(t + 1) * low, :] = block.astype(BF16)
    for n in range(mid * low // 512):
        if n % 4 == 0:
            loads[n // 4].wait()
        at = n * 512
        both = dot(diag[...], jnp.concatenate([held[at:at + 256, :], held[at + 256:at + 512, :]], axis=1))
        for t in range(2 * times):
            to = (n * 2 * times + t) * PITCH
            side = t // times * LANES
            at = t % times * low
            rows_f[to:to + low, :] = both[at:at + low, side:side + LANES]
    for copy in others:
        copy.wait()
    scaled = column_of_row(row[pl.ds(lax.rem(place, 8), 1), :]) * wide[...].astype(F32)
    profile = kernel_low[...].astype(F32)
    turned = pltpu.roll(profile, HALF, 1)
    stores = []
    for k in range(low):
        matrix = (scaled * twist[k:k + 1, :]).astype(BF16)
        second = dot(matrix, rows_f[pl.ds(k, mid, stride=PITCH), :].astype(BF16))
        halves = trade_halves(second[:HALF], second[HALF:])
        for h, (half, line) in enumerate(zip(halves, (profile, turned))):
            to = (2 * k + h) * PITCH
            out[to:to + HALF, :] = half.astype(BF16)
            out[to + HALF:to + PITCH, :] = jnp.broadcast_to(line[k:k + 1, :], (PITCH - HALF, LANES)).astype(BF16)
        if k % 16 == 15:
            size = 32 * PITCH
            at = k // 16 * size
            store = pltpu.make_async_copy(
                out.at[pl.ds(at, size)], message.at[pl.ds(at, size)], sem_out.at[k // 16]
            )
            store.start()
            stores.append(store)
    for store in stores:
        store.wait()


def middle_kernel(columns, kernel_top, packed, third,
                  out, rows_f, rows_g, whole, lines, sem_out):
    top = kernel_top.shape[0]
    factor_top, inverse_top, inverse_mid = (packed.at[pl.ds((HALF + n) * top, top)] for n in range(3))
    place = lax.axis_index("seq")
    for n in range(top // 8):
        at = n * 8 * PITCH
        rows_f[at:at + 8 * PITCH, :] = columns[at:at + 8 * PITCH, :].astype(F32)
    rows = rows_f[pl.ds(HALF, 2 * HALF, stride=PITCH), :]
    lines[...] = trade_halves(rows[:HALF], rows[HALF:])[0]
    lower = iota((top, LANES), 1) < HALF
    all_top = kernel_top[...]
    turned = pltpu.roll(all_top, HALF, 1)
    keep = lower == (lax.rem(place, 2) == 0)
    whole[...] = jnp.where(keep, all_top, turned)

    for r in range(0, HALF, 2):
        one = rows_f[pl.ds(r, top, stride=PITCH), :].astype(BF16)
        two = rows_f[pl.ds(r + 1, top, stride=PITCH), :].astype(BF16)
        spectrum = dot(factor_top[...], jnp.concatenate([one, two], axis=1)).astype(BF16).astype(F32)
        first = spectrum[:, :LANES] * whole[...] * lines[r:r + 1, :]
        other = spectrum[:, LANES:] * whole[...] * lines[r + 1:r + 2, :]
        filtered = jnp.concatenate([first.astype(BF16), other.astype(BF16)], axis=1)
        back = dot(inverse_top[...], filtered)
        rows_g[pl.ds(r, top, stride=PITCH), :] = back[:, :LANES] * packed[r * top:(r + 1) * top, :].astype(F32)
        rows_g[pl.ds(r + 1, top, stride=PITCH), :] = back[:, LANES:] * packed[(r + 1) * top:(r + 2) * top, :].astype(F32)

    part = 32 * HALF
    stores = []
    for n in range(top // 4):
        sides = []
        for m in range(2):
            at = (n * 4 + m * 2) * PITCH
            upper, under = trade_halves(rows_g[at:at + HALF, :], rows_g[at + PITCH:at + PITCH + HALF, :])
            sides.append(jnp.concatenate([upper.astype(BF16), under.astype(BF16)], axis=0))
        result = dot(inverse_mid[...], jnp.concatenate(sides, axis=1))
        for m in range(2):
            side = result[:, m * LANES:(m + 1) * LANES]
            for q in range(4):
                pair = trade_halves(side[q * 32:q * 32 + 16], side[q * 32 + 16:q * 32 + 32])
                for p in range(2):
                    to = (n * 4 + m * 2 + p) * HALF + q * 16
                    out[to:to + 16, :] = pair[p].astype(BF16)
        if n % 8 == 7:
            at = n // 8 * part
            store = pltpu.make_async_copy(out.at[pl.ds(at, part)], third.at[pl.ds(at, part)], sem_out.at[n // 8])
            store.start()
            stores.append(store)
    for store in stores:
        store.wait()


def pack_kernel(untwist_top, factor_top, inverse_top, inverse_mid, untwist_low, packed):
    top = untwist_top.shape[0]
    place = lax.axis_index("seq")
    shape = (top, LANES)
    lower = iota(shape, 1) < HALF
    for r in range(HALF):
        one = jnp.broadcast_to(untwist_top[:, r:r + 1], shape)
        two = jnp.broadcast_to(untwist_top[:, HALF + r:HALF + r + 1], shape)
        packed[r * top:(r + 1) * top, :] = jnp.where(lower, one, two).astype(BF16)
    at = HALF * top
    packed[at:at + top, :] = factor_top[...]
    packed[at + top:at + 2 * top, :] = inverse_top[...]
    column = column_of_row(untwist_low[pl.ds(place // 2, 1), :])
    packed[at + 2 * top:at + 3 * top, :] = (column * inverse_mid[...].astype(F32)).astype(BF16)


def silu_kernel(*refs):
    sources, target = refs[:-1], refs[-1]
    for t, source in enumerate(sources):
        def body(n, _):
            at = pl.multiple_of(n * 256, 256)
            value = source[pl.ds(at, 256), :].astype(F32)
            target[t, pl.ds(at, 256), :] = ((0.5 * value) * (1.0 + jnp.tanh(0.5 * value))).astype(BF16)
            return 0

        lax.fori_loop(0, source.shape[0] // 256, body, 0)


def last_kernel(low, third, inverse_low, silu, *refs):
    weights, out, rows_f, gated, result, sem_out = refs[:4], *refs[4:]
    pitch = LANES + 8
    block = 4 * low
    place = lax.axis_index("ch")
    for k in range(low):
        for h in range(2):
            for t in range(4):
                source = pl.multiple_of(((k * 2 + h) * 4 + (place ^ t)) * 16, 16)
                to = k * pitch + (h * 4 + t) * 16
                rows_f[to:to + 16, :] = third[pl.ds(source, 16), :].astype(F32)
    copies = []
    for g in range(4):
        for b in range(4 * g, 4 * g + 4):
            for t in range(4):
                one = rows_f[pl.ds(t * 16 + b, low, stride=pitch), :]
                two = rows_f[pl.ds((4 + t) * 16 + b, low, stride=pitch), :]
                pair = trade_halves(one, two)
                mixed = dot(inverse_low[...], jnp.concatenate([p.astype(BF16) for p in pair], axis=1))
                for p in range(2):
                    at = (p * 16 + b) * low
                    gated[at:at + low, t * LANES:(t + 1) * LANES] = (
                        mixed[:, p * LANES:(p + 1) * LANES] * silu[t, at:at + low, :].astype(F32)
                    ).astype(BF16)
        for p in range(2):
            at = (p * 4 + g) * block
            total = dot(gated[at:at + block, :LANES], weights[0][...])
            for t in range(1, 4):
                total += dot(gated[at:at + block, t * LANES:(t + 1) * LANES], weights[t][...])
            result[at:at + block, :] = total.astype(BF16)
            copy = pltpu.make_async_copy(
                result.at[pl.ds(at, block)], out.at[pl.ds(at, block)], sem_out.at[g * 2 + p]
            )
            copy.start()
            copies.append(copy)
    for copy in copies:
        copy.wait()


def call(kernel, name, out_shape, scratch, flops, *args, limit=40 << 20, far=(), out_spec=None):
    vmem, hbm = pl.BlockSpec(memory_space=pltpu.VMEM), pl.BlockSpec(memory_space=pl.ANY)
    outs = jax.tree.leaves(out_shape)
    moved = sum(a.size * a.dtype.itemsize for a in args) + sum(o.size * o.dtype.itemsize for o in outs)
    return pl.pallas_call(
        kernel,
        name=name,
        out_shape=out_shape,
        in_specs=[hbm if n in far else vmem for n in range(len(args))],
        out_specs=jax.tree.map(lambda _: out_spec or vmem, out_shape),
        scratch_shapes=scratch,
        compiler_params=pltpu.CompilerParams(vmem_limit_bytes=limit),
        cost_estimate=pl.CostEstimate(flops=flops, bytes_accessed=moved, transcendentals=0),
    )(*args)


def local(
    values,
    factor_low,
    twist_low,
    factor_mid,
    twist_top,
    factor_top,
    kernel_top,
    kernel_low,
    inverse_top,
    untwist_top,
    inverse_mid,
    untwist_low,
    inverse_low,
    out_weight,
):
    low = factor_low.shape[0]
    mid = factor_mid.shape[0]
    top = factor_top.shape[0]
    rows, width = values.shape
    ch_place = lax.axis_index("ch")
    ch_count = lax.axis_size("ch")
    share = rows // ch_count
    columns_out = out_weight.shape[1]
    unit = 2 * rows * width
    padded = pltpu.VMEM((top * PITCH, width), F32)

    def swap(array, turn):
        if turn == 0:
            return array
        return lax.ppermute(array, "ch", [(c, c ^ turn) for c in range(ch_count)])

    message = call(
        functools.partial(forward_kernel, low), "forward", jax.ShapeDtypeStruct((2 * low * PITCH, width), BF16),
        [
            pltpu.VMEM((rows, width), BF16),
            pltpu.VMEM((low, low), BF16),
            pltpu.VMEM((mid, mid), BF16),
            pltpu.VMEM((8, mid), F32),
            pltpu.VMEM((low, mid), F32),
            padded,
            pltpu.VMEM((256, 256), BF16),
            pltpu.VMEM((2 * low * PITCH, width), BF16),
            pltpu.SemaphoreType.DMA((8,)),
            pltpu.SemaphoreType.DMA((4,)),
        ], unit * (low + mid),
        values, factor_low, twist_low.T, factor_mid, twist_top, kernel_low,
        limit=60 << 20, far=range(5), out_spec=pl.BlockSpec(memory_space=pl.ANY),
    )
    message, untwist_t = lax.optimization_barrier((message, untwist_top))
    columns = lax.all_to_all(message.reshape(2 * low, PITCH, width), "seq", 0, 0, tiled=True)

    turns = range(ch_count)
    shares = [lax.dynamic_slice_in_dim(values, (ch_place ^ turn) * share, share, 0) for turn in turns]
    shares = [swap(array, turn) if turn < 3 else array for turn, array in enumerate(shares)]
    packed = call(
        pack_kernel, "pack", jax.ShapeDtypeStruct(((HALF + 3) * top, width), BF16), [], unit,
        untwist_t, factor_top, inverse_top, inverse_mid, untwist_low.T, limit=8 << 20,
    )
    columns, shares = lax.optimization_barrier((columns, shares))
    third = call(
        middle_kernel, "middle", jax.ShapeDtypeStruct((rows, width), BF16),
        [
            pltpu.VMEM((rows, width), BF16),
            padded,
            padded,
            pltpu.VMEM((top, width), F32),
            pltpu.VMEM((HALF, width), F32),
            pltpu.SemaphoreType.DMA((4,)),
        ], unit * (2 * top + mid),
        columns.reshape(top * PITCH, width), kernel_top, packed, limit=24 << 20, out_spec=pl.BlockSpec(memory_space=pltpu.HBM),
    )
    third, shares, out_weight = lax.optimization_barrier((third, shares, out_weight))
    shares = [swap(array, turn) if turn == 3 else array for turn, array in enumerate(shares)]
    weights = [swap(out_weight, turn) for turn in turns]
    silu = call(
        silu_kernel, "silu", jax.ShapeDtypeStruct((ch_count, share, width), BF16), [], unit, *shares, limit=12 << 20
    )
    third = lax.all_to_all(third.reshape(top * ch_count, -1, width), ("seq", "ch"), 0, 0, tiled=True)
    return call(
        functools.partial(last_kernel, low), "last", jax.ShapeDtypeStruct((share, columns_out), BF16),
        [
            pltpu.VMEM((low * (width + 8), width), F32),
            pltpu.VMEM((share, columns_out), BF16),
            pltpu.VMEM((share, columns_out), BF16),
            pltpu.SemaphoreType.DMA((8,)),
        ],
        unit * low // 2 + 2 * share * columns_out ** 2,
        third.reshape(rows, width), inverse_low, silu, *weights,
        limit=24 << 20, out_spec=pl.BlockSpec(memory_space=pltpu.HBM),
    )


def solution(mesh):
    return jax.shard_map(
        local,
        mesh=mesh,
        in_specs=(
            P("seq", "ch"),
            P(),
            P(),
            P(),
            P(),
            P(),
            P(None, "ch"),
            P("seq", "ch"),
            P(),
            P(),
            P(),
            P(),
            P(),
            P("ch", None),
        ),
        out_specs=P(("seq", "ch"), None),
        check_vma=False,
    )
```

```python
import functools

import jax
import jax.numpy as jnp
from jax import lax
from jax.experimental import pallas as pl
from jax.experimental.pallas import tpu as pltpu
from jax.sharding import PartitionSpec as P

F32 = jnp.float32
BF16 = jnp.bfloat16
LANES = 128
HALF = 64
PITCH = 72


def iota(shape, axis):
    return lax.broadcasted_iota(jnp.int32, shape, axis)


def dot(left, right):
    return jnp.dot(left, right, preferred_element_type=F32)


def repeat_lanes(matrix, times):
    n = matrix.shape[1]
    shape = (n, n * times)
    pick = (lax.rem(iota(shape, 1), n) == iota(shape, 0)).astype(F32).astype(BF16)
    return dot(matrix, pick)


def column_of_row(row):
    n = row.shape[1]
    square = jnp.broadcast_to(row, (n, n))
    return jnp.sum(jnp.where(iota((n, n), 0) == iota((n, n), 1), square, 0.0), axis=1, keepdims=True)


def trade_halves(one, two):
    low = iota(one.shape, 1) < HALF
    return jnp.where(low, one, pltpu.roll(two, HALF, 1)), jnp.where(low, pltpu.roll(one, HALF, 1), two)


def forward_kernel(low, values, factor_low, twist_low, factor_mid, twist_top, kernel_low, message,
                   rows_f, diag, out, sem_out):
    mid = factor_mid.shape[0]
    times = 256 // low
    place = lax.axis_index("seq")
    tiled = repeat_lanes(factor_low[...], times)
    for t in range(times):
        block = jnp.where(iota(tiled.shape, 1) // low == t, tiled, 0.0)
        diag[t * low:(t + 1) * low, :] = block.astype(BF16)
    for n in range(mid * low // 512):
        at = n * 512
        both = dot(diag[...], jnp.concatenate([values[at:at + 256, :], values[at + 256:at + 512, :]], axis=1))
        for t in range(2 * times):
            to = (n * 2 * times + t) * PITCH
            side = t // times * LANES
            at = t % times * low
            rows_f[to:to + low, :] = both[at:at + low, side:side + LANES]
    scaled = column_of_row(twist_top[pl.ds(place, 1), :]) * factor_mid[...].astype(F32)
    profile = kernel_low[...].astype(F32)
    turned = pltpu.roll(profile, HALF, 1)
    stores = []
    for k in range(low):
        matrix = (scaled * twist_low[k:k + 1, :]).astype(BF16)
        second = dot(matrix, rows_f[pl.ds(k, mid, stride=PITCH), :].astype(BF16))
        halves = trade_halves(second[:HALF], second[HALF:])
        for h, (half, line) in enumerate(zip(halves, (profile, turned))):
            to = (2 * k + h) * PITCH
            out[to:to + HALF, :] = half.astype(BF16)
            out[to + HALF:to + PITCH, :] = jnp.broadcast_to(line[k:k + 1, :], (PITCH - HALF, LANES)).astype(BF16)
        if k % 16 == 15:
            size = 32 * PITCH
            at = k // 16 * size
            store = pltpu.make_async_copy(
                out.at[pl.ds(at, size)], message.at[pl.ds(at, size)], sem_out.at[k // 16]
            )
            store.start()
            stores.append(store)
    for store in stores:
        store.wait()


def middle_kernel(columns, kernel_top, packed, third,
                  out, rows_f, rows_g, whole, lines, sem_out):
    top = kernel_top.shape[0]
    factor_top, inverse_top, inverse_mid = (packed.at[pl.ds((HALF + n) * top, top)] for n in range(3))
    place = lax.axis_index("seq")
    for n in range(top // 8):
        at = n * 8 * PITCH
        rows_f[at:at + 8 * PITCH, :] = columns[at:at + 8 * PITCH, :].astype(F32)
    rows = rows_f[pl.ds(HALF, 2 * HALF, stride=PITCH), :]
    lines[...] = trade_halves(rows[:HALF], rows[HALF:])[0]
    lower = iota((top, LANES), 1) < HALF
    all_top = kernel_top[...]
    turned = pltpu.roll(all_top, HALF, 1)
    keep = lower == (lax.rem(place, 2) == 0)
    whole[...] = jnp.where(keep, all_top, turned)

    for r in range(0, HALF, 2):
        one = rows_f[pl.ds(r, top, stride=PITCH), :].astype(BF16)
        two = rows_f[pl.ds(r + 1, top, stride=PITCH), :].astype(BF16)
        spectrum = dot(factor_top[...], jnp.concatenate([one, two], axis=1)).astype(BF16).astype(F32)
        first = spectrum[:, :LANES] * whole[...] * lines[r:r + 1, :]
        other = spectrum[:, LANES:] * whole[...] * lines[r + 1:r + 2, :]
        filtered = jnp.concatenate([first.astype(BF16), other.astype(BF16)], axis=1)
        back = dot(inverse_top[...], filtered)
        rows_g[pl.ds(r, top, stride=PITCH), :] = back[:, :LANES] * packed[r * top:(r + 1) * top, :].astype(F32)
        rows_g[pl.ds(r + 1, top, stride=PITCH), :] = back[:, LANES:] * packed[(r + 1) * top:(r + 2) * top, :].astype(F32)

    part = 32 * HALF
    stores = []
    for n in range(top // 4):
        sides = []
        for m in range(2):
            at = (n * 4 + m * 2) * PITCH
            upper, under = trade_halves(rows_g[at:at + HALF, :], rows_g[at + PITCH:at + PITCH + HALF, :])
            sides.append(jnp.concatenate([upper.astype(BF16), under.astype(BF16)], axis=0))
        result = dot(inverse_mid[...], jnp.concatenate(sides, axis=1))
        for m in range(2):
            side = result[:, m * LANES:(m + 1) * LANES]
            for q in range(4):
                pair = trade_halves(side[q * 32:q * 32 + 16], side[q * 32 + 16:q * 32 + 32])
                for p in range(2):
                    to = (n * 4 + m * 2 + p) * HALF + q * 16
                    out[to:to + 16, :] = pair[p].astype(BF16)
        if n % 8 == 7:
            at = n // 8 * part
            store = pltpu.make_async_copy(out.at[pl.ds(at, part)], third.at[pl.ds(at, part)], sem_out.at[n // 8])
            store.start()
            stores.append(store)
    for store in stores:
        store.wait()


def pack_kernel(untwist_top, factor_top, inverse_top, inverse_mid, untwist_low, packed):
    top = untwist_top.shape[0]
    place = lax.axis_index("seq")
    shape = (top, LANES)
    lower = iota(shape, 1) < HALF
    for r in range(HALF):
        one = jnp.broadcast_to(untwist_top[:, r:r + 1], shape)
        two = jnp.broadcast_to(untwist_top[:, HALF + r:HALF + r + 1], shape)
        packed[r * top:(r + 1) * top, :] = jnp.where(lower, one, two).astype(BF16)
    at = HALF * top
    packed[at:at + top, :] = factor_top[...]
    packed[at + top:at + 2 * top, :] = inverse_top[...]
    column = column_of_row(untwist_low[pl.ds(place // 2, 1), :])
    packed[at + 2 * top:at + 3 * top, :] = (column * inverse_mid[...].astype(F32)).astype(BF16)


def gate_kernel(*refs):
    sources, weights, (target, matrix) = refs[:4], refs[4:8], refs[8:]
    for t, (source, weight) in enumerate(zip(sources, weights)):
        matrix[t * LANES:(t + 1) * LANES, :] = weight[...]

        def body(n, _):
            at = pl.multiple_of(n * 256, 256)
            value = source[pl.ds(at, 256), :].astype(F32)
            gate = ((0.5 * value) * (1.0 + jnp.tanh(0.5 * value))).astype(BF16)
            target[pl.ds(at, 256), t * LANES:(t + 1) * LANES] = gate
            return 0

        lax.fori_loop(0, source.shape[0] // 256, body, 0)


def last_kernel(low, third, inverse_low, silu, matrix, out, gates, rows_f, gated, result, sem_in, sem_out):
    pitch = LANES + 8
    block = 4 * low
    place = lax.axis_index("ch")
    fetches = [
        pltpu.make_async_copy(silu.at[pl.ds(at, block)], gates.at[pl.ds(at, block)], sem_in.at[n])
        for n, at in enumerate((p * 4 + g) * block for g in range(4) for p in range(2))
    ]
    for copy in fetches:
        copy.start()
    for k in range(low):
        for h in range(2):
            for t in range(4):
                source = pl.multiple_of(((k * 2 + h) * 4 + (place ^ t)) * 16, 16)
                to = k * pitch + (h * 4 + t) * 16
                rows_f[to:to + 16, :] = third[pl.ds(source, 16), :].astype(F32)
    copies = []
    for copy in fetches:
        copy.wait()
    for g in range(4):
        for b in range(4 * g, 4 * g + 4):
            for t in range(4):
                one = rows_f[pl.ds(t * 16 + b, low, stride=pitch), :]
                two = rows_f[pl.ds((4 + t) * 16 + b, low, stride=pitch), :]
                pair = trade_halves(one, two)
                mixed = dot(inverse_low[...], jnp.concatenate([p.astype(BF16) for p in pair], axis=1))
                for p in range(2):
                    at = (p * 16 + b) * low
                    gated[at:at + low, t * LANES:(t + 1) * LANES] = (
                        mixed[:, p * LANES:(p + 1) * LANES] * gates[at:at + low, t * LANES:(t + 1) * LANES].astype(F32)
                    ).astype(BF16)
        for p in range(2):
            at = (p * 4 + g) * block
            total = dot(gated[at:at + block, :], matrix[...])
            result[at:at + block, :] = total.astype(BF16)
            copy = pltpu.make_async_copy(
                result.at[pl.ds(at, block)], out.at[pl.ds(at, block)], sem_out.at[g * 2 + p]
            )
            copy.start()
            copies.append(copy)
    for copy in copies:
        copy.wait()


def call(kernel, name, out_shape, scratch, flops, *args, limit=40 << 20, far=(), out_spec=None, aliases=None):
    vmem, hbm = pl.BlockSpec(memory_space=pltpu.VMEM), pl.BlockSpec(memory_space=pl.ANY)
    outs = jax.tree.leaves(out_shape)
    moved = sum(a.size * a.dtype.itemsize for a in args) + sum(o.size * o.dtype.itemsize for o in outs)
    return pl.pallas_call(
        kernel,
        name=name,
        out_shape=out_shape,
        in_specs=[hbm if n in far else vmem for n in range(len(args))],
        out_specs=jax.tree.map(lambda _: out_spec or vmem, out_shape),
        scratch_shapes=scratch,
        input_output_aliases=aliases or {},
        compiler_params=pltpu.CompilerParams(vmem_limit_bytes=limit),
        cost_estimate=pl.CostEstimate(flops=flops, bytes_accessed=moved, transcendentals=0),
    )(*args)


def local(
    values,
    factor_low,
    twist_low,
    factor_mid,
    twist_top,
    factor_top,
    kernel_top,
    kernel_low,
    inverse_top,
    untwist_top,
    inverse_mid,
    untwist_low,
    inverse_low,
    out_weight,
):
    low = factor_low.shape[0]
    mid = factor_mid.shape[0]
    top = factor_top.shape[0]
    rows, width = values.shape
    ch_place = lax.axis_index("ch")
    ch_count = lax.axis_size("ch")
    share = rows // ch_count
    columns_out = out_weight.shape[1]
    unit = 2 * rows * width
    padded = pltpu.VMEM((top * PITCH, width), F32)

    def swap(array, turn):
        if turn == 0:
            return array
        return lax.ppermute(array, "ch", [(c, c ^ turn) for c in range(ch_count)])

    message = call(
        functools.partial(forward_kernel, low), "forward", jax.ShapeDtypeStruct((2 * low * PITCH, width), BF16),
        [
            padded,
            pltpu.VMEM((256, 256), BF16),
            pltpu.VMEM((2 * low * PITCH, width), BF16),
            pltpu.SemaphoreType.DMA((4,)),
        ], unit * (low + mid),
        values, factor_low, twist_low.T, factor_mid, twist_top, kernel_low,
        limit=60 << 20, out_spec=pl.BlockSpec(memory_space=pl.ANY),
    )
    message, untwist_t = lax.optimization_barrier((message, untwist_top))
    columns = lax.all_to_all(message.reshape(2 * low, PITCH, width), "seq", 0, 0, tiled=True)

    turns = range(ch_count)
    shares = [lax.dynamic_slice_in_dim(values, (ch_place ^ turn) * share, share, 0) for turn in turns]
    shares = [swap(array, turn) if turn < 3 else array for turn, array in enumerate(shares)]
    packed = call(
        pack_kernel, "pack", jax.ShapeDtypeStruct(((HALF + 3) * top, width), BF16), [], unit,
        untwist_t, factor_top, inverse_top, inverse_mid, untwist_low.T, limit=8 << 20,
    )
    columns, shares = lax.optimization_barrier((columns, shares))
    third = call(
        middle_kernel, "middle", jax.ShapeDtypeStruct((rows, width), BF16),
        [
            pltpu.VMEM((rows, width), BF16),
            padded,
            padded,
            pltpu.VMEM((top, width), F32),
            pltpu.VMEM((HALF, width), F32),
            pltpu.SemaphoreType.DMA((4,)),
        ], unit * (2 * top + mid),
        columns.reshape(top * PITCH, width), kernel_top, packed, limit=24 << 20, out_spec=pl.BlockSpec(memory_space=pltpu.HBM),
    )
    third, shares, out_weight = lax.optimization_barrier((third, shares, out_weight))
    shares = [swap(array, turn) if turn == 3 else array for turn, array in enumerate(shares)]
    weights = [swap(out_weight, turn) for turn in turns]
    silu, matrix = call(
        gate_kernel, "gate",
        [jax.ShapeDtypeStruct((share, columns_out), BF16), jax.ShapeDtypeStruct((ch_count * width, columns_out), BF16)],
        [], unit, *shares, *weights, limit=12 << 20,
    )
    third = lax.all_to_all(third.reshape(top * ch_count, -1, width), ("seq", "ch"), 0, 0, tiled=True)
    return call(
        functools.partial(last_kernel, low), "last", jax.ShapeDtypeStruct((share, columns_out), BF16),
        [
            pltpu.VMEM((share, columns_out), BF16),
            pltpu.VMEM((low * (width + 8), width), F32),
            pltpu.VMEM((share, columns_out), BF16),
            pltpu.VMEM((share, columns_out), BF16),
            pltpu.SemaphoreType.DMA((8,)),
            pltpu.SemaphoreType.DMA((8,)),
        ],
        unit * low // 2 + 2 * share * columns_out ** 2,
        third.reshape(rows, width), inverse_low, silu, matrix,
        limit=24 << 20, far=(2,), out_spec=pl.BlockSpec(memory_space=pl.ANY), aliases={2: 0},
    )


def solution(mesh):
    return jax.shard_map(
        local,
        mesh=mesh,
        in_specs=(
            P("seq", "ch"),
            P(),
            P(),
            P(),
            P(),
            P(),
            P(None, "ch"),
            P("seq", "ch"),
            P(),
            P(),
            P(),
            P(),
            P(),
            P("ch", None),
        ),
        out_specs=P(("seq", "ch"), None),
        check_vma=False,
    )
```

```python
import functools

import jax
import jax.numpy as jnp
from jax import lax
from jax.experimental import pallas as pl
from jax.experimental.pallas import tpu as pltpu
from jax.sharding import PartitionSpec as P

F32 = jnp.float32
BF16 = jnp.bfloat16
LANES = 128
HALF = 64
PITCH = 72


def iota(shape, axis):
    return lax.broadcasted_iota(jnp.int32, shape, axis)


def dot(left, right):
    return jnp.dot(left, right, preferred_element_type=F32)


def repeat_lanes(matrix, times):
    n = matrix.shape[1]
    shape = (n, n * times)
    pick = (lax.rem(iota(shape, 1), n) == iota(shape, 0)).astype(F32).astype(BF16)
    return dot(matrix, pick)


def column_of_row(row):
    n = row.shape[1]
    square = jnp.broadcast_to(row, (n, n))
    return jnp.sum(jnp.where(iota((n, n), 0) == iota((n, n), 1), square, 0.0), axis=1, keepdims=True)


def trade_halves(one, two):
    low = iota(one.shape, 1) < HALF
    return jnp.where(low, one, pltpu.roll(two, HALF, 1)), jnp.where(low, pltpu.roll(one, HALF, 1), two)


def forward_kernel(low, values, factor_low, twist_low, factor_mid, twist_top, kernel_low, message,
                   rows_f, diag, out, sem_out):
    mid = factor_mid.shape[0]
    times = 256 // low
    place = lax.axis_index("seq")
    tiled = repeat_lanes(factor_low[...], times)
    for t in range(times):
        block = jnp.where(iota(tiled.shape, 1) // low == t, tiled, 0.0)
        diag[t * low:(t + 1) * low, :] = block.astype(BF16)
    for n in range(mid * low // 512):
        at = n * 512
        both = dot(diag[...], jnp.concatenate([values[at:at + 256, :], values[at + 256:at + 512, :]], axis=1))
        for t in range(2 * times):
            to = (n * 2 * times + t) * PITCH
            side = t // times * LANES
            at = t % times * low
            rows_f[to:to + low, :] = both[at:at + low, side:side + LANES]
    scaled = column_of_row(twist_top[pl.ds(place, 1), :]) * factor_mid[...].astype(F32)
    profile = kernel_low[...].astype(F32)
    turned = pltpu.roll(profile, HALF, 1)
    stores = []
    for k in range(low):
        matrix = (scaled * twist_low[k:k + 1, :]).astype(BF16)
        second = dot(matrix, rows_f[pl.ds(k, mid, stride=PITCH), :].astype(BF16))
        halves = trade_halves(second[:HALF], second[HALF:])
        for h, (half, line) in enumerate(zip(halves, (profile, turned))):
            to = (2 * k + h) * PITCH
            out[to:to + HALF, :] = half.astype(BF16)
            out[to + HALF:to + PITCH, :] = jnp.broadcast_to(line[k:k + 1, :], (PITCH - HALF, LANES)).astype(BF16)
        if k % 16 == 15:
            size = 32 * PITCH
            at = k // 16 * size
            store = pltpu.make_async_copy(
                out.at[pl.ds(at, size)], message.at[pl.ds(at, size)], sem_out.at[k // 16]
            )
            store.start()
            stores.append(store)
    for store in stores:
        store.wait()


def middle_kernel(columns, kernel_top, packed, third,
                  out, rows_f, rows_g, whole, lines, sem_out):
    top = kernel_top.shape[0]
    factor_top, inverse_top, inverse_mid = (packed.at[pl.ds((HALF + n) * top, top)] for n in range(3))
    place = lax.axis_index("seq")
    for n in range(top // 8):
        at = n * 8 * PITCH
        rows_f[at:at + 8 * PITCH, :] = columns[at:at + 8 * PITCH, :].astype(F32)
    rows = rows_f[pl.ds(HALF, 2 * HALF, stride=PITCH), :]
    lines[...] = trade_halves(rows[:HALF], rows[HALF:])[0]
    lower = iota((top, LANES), 1) < HALF
    all_top = kernel_top[...]
    turned = pltpu.roll(all_top, HALF, 1)
    keep = lower == (lax.rem(place, 2) == 0)
    whole[...] = jnp.where(keep, all_top, turned)

    for r in range(0, HALF, 2):
        one = rows_f[pl.ds(r, top, stride=PITCH), :].astype(BF16)
        two = rows_f[pl.ds(r + 1, top, stride=PITCH), :].astype(BF16)
        spectrum = dot(factor_top[...], jnp.concatenate([one, two], axis=1)).astype(BF16).astype(F32)
        first = spectrum[:, :LANES] * whole[...] * lines[r:r + 1, :]
        other = spectrum[:, LANES:] * whole[...] * lines[r + 1:r + 2, :]
        filtered = jnp.concatenate([first.astype(BF16), other.astype(BF16)], axis=1)
        back = dot(inverse_top[...], filtered)
        rows_g[pl.ds(r, top, stride=PITCH), :] = back[:, :LANES] * packed[r * top:(r + 1) * top, :].astype(F32)
        rows_g[pl.ds(r + 1, top, stride=PITCH), :] = back[:, LANES:] * packed[(r + 1) * top:(r + 2) * top, :].astype(F32)

    part = 32 * HALF
    stores = []
    for n in range(top // 4):
        sides = []
        for m in range(2):
            at = (n * 4 + m * 2) * PITCH
            upper, under = trade_halves(rows_g[at:at + HALF, :], rows_g[at + PITCH:at + PITCH + HALF, :])
            sides.append(jnp.concatenate([upper.astype(BF16), under.astype(BF16)], axis=0))
        result = dot(inverse_mid[...], jnp.concatenate(sides, axis=1))
        for m in range(2):
            side = result[:, m * LANES:(m + 1) * LANES]
            for q in range(4):
                pair = trade_halves(side[q * 32:q * 32 + 16], side[q * 32 + 16:q * 32 + 32])
                for p in range(2):
                    to = (n * 4 + m * 2 + p) * HALF + q * 16
                    out[to:to + 16, :] = pair[p].astype(BF16)
        if n % 8 == 7:
            at = n // 8 * part
            store = pltpu.make_async_copy(out.at[pl.ds(at, part)], third.at[pl.ds(at, part)], sem_out.at[n // 8])
            store.start()
            stores.append(store)
    for store in stores:
        store.wait()


def pack_kernel(untwist_top, factor_top, inverse_top, inverse_mid, untwist_low, packed):
    top = untwist_top.shape[0]
    place = lax.axis_index("seq")
    shape = (top, LANES)
    lower = iota(shape, 1) < HALF
    for r in range(HALF):
        one = jnp.broadcast_to(untwist_top[:, r:r + 1], shape)
        two = jnp.broadcast_to(untwist_top[:, HALF + r:HALF + r + 1], shape)
        packed[r * top:(r + 1) * top, :] = jnp.where(lower, one, two).astype(BF16)
    at = HALF * top
    packed[at:at + top, :] = factor_top[...]
    packed[at + top:at + 2 * top, :] = inverse_top[...]
    column = column_of_row(untwist_low[pl.ds(place // 2, 1), :])
    packed[at + 2 * top:at + 3 * top, :] = (column * inverse_mid[...].astype(F32)).astype(BF16)


def gate_kernel(*refs):
    sources, weights, (target, matrix) = refs[:4], refs[4:8], refs[8:]
    for t, (source, weight) in enumerate(zip(sources, weights)):
        matrix[t * LANES:(t + 1) * LANES, :] = weight[...]

        def body(n, _):
            at = pl.multiple_of(n * 256, 256)
            value = source[pl.ds(at, 256), :].astype(F32)
            gate = ((0.5 * value) * (1.0 + jnp.tanh(0.5 * value))).astype(BF16)
            target[pl.ds(at, 256), t * LANES:(t + 1) * LANES] = gate
            return 0

        lax.fori_loop(0, source.shape[0] // 256, body, 0)


def last_kernel(low, third, inverse_low, silu, matrix, out, gates, rows_f, gated, result, sem_in, sem_out):
    pitch = LANES + 8
    block = 4 * low
    place = lax.axis_index("ch")
    fetches = [
        pltpu.make_async_copy(silu.at[pl.ds(at, block)], gates.at[pl.ds(at, block)], sem_in.at[n])
        for n, at in enumerate((p * 4 + g) * block for g in range(4) for p in range(2))
    ]
    for copy in fetches:
        copy.start()
    for k in range(low):
        for h in range(2):
            for t in range(4):
                source = pl.multiple_of(((k * 2 + h) * 4 + (place ^ t)) * 16, 16)
                to = k * pitch + (h * 4 + t) * 16
                rows_f[to:to + 16, :] = third[pl.ds(source, 16), :].astype(F32)
    copies = []
    for copy in fetches:
        copy.wait()
    for g in range(4):
        for b in range(4 * g, 4 * g + 4):
            for t in range(4):
                one = rows_f[pl.ds(t * 16 + b, low, stride=pitch), :]
                two = rows_f[pl.ds((4 + t) * 16 + b, low, stride=pitch), :]
                pair = trade_halves(one, two)
                mixed = dot(inverse_low[...], jnp.concatenate([p.astype(BF16) for p in pair], axis=1))
                for p in range(2):
                    at = (p * 16 + b) * low
                    gated[at:at + low, t * LANES:(t + 1) * LANES] = (
                        mixed[:, p * LANES:(p + 1) * LANES] * gates[at:at + low, t * LANES:(t + 1) * LANES].astype(F32)
                    ).astype(BF16)
        for p in range(2):
            at = (p * 4 + g) * block
            total = dot(gated[at:at + block, :], matrix[...])
            result[at:at + block, :] = total.astype(BF16)
            copy = pltpu.make_async_copy(
                result.at[pl.ds(at, block)], out.at[pl.ds(at, block)], sem_out.at[g * 2 + p]
            )
            copy.start()
            copies.append(copy)
    for copy in copies:
        copy.wait()


def call(kernel, name, out_shape, scratch, flops, *args, limit=40 << 20, far=(), out_spec=None, aliases=None):
    vmem, hbm = pl.BlockSpec(memory_space=pltpu.VMEM), pl.BlockSpec(memory_space=pl.ANY)
    outs = jax.tree.leaves(out_shape)
    moved = sum(a.size * a.dtype.itemsize for a in args) + sum(o.size * o.dtype.itemsize for o in outs)
    return pl.pallas_call(
        kernel,
        name=name,
        out_shape=out_shape,
        in_specs=[hbm if n in far else vmem for n in range(len(args))],
        out_specs=jax.tree.map(lambda _: out_spec or vmem, out_shape),
        scratch_shapes=scratch,
        input_output_aliases=aliases or {},
        compiler_params=pltpu.CompilerParams(vmem_limit_bytes=limit),
        cost_estimate=pl.CostEstimate(flops=flops, bytes_accessed=moved, transcendentals=0),
    )(*args)


def local(
    values,
    factor_low,
    twist_low,
    factor_mid,
    twist_top,
    factor_top,
    kernel_top,
    kernel_low,
    inverse_top,
    untwist_top,
    inverse_mid,
    untwist_low,
    inverse_low,
    out_weight,
):
    low = factor_low.shape[0]
    mid = factor_mid.shape[0]
    top = factor_top.shape[0]
    rows, width = values.shape
    ch_place = lax.axis_index("ch")
    ch_count = lax.axis_size("ch")
    share = rows // ch_count
    columns_out = out_weight.shape[1]
    unit = 2 * rows * width
    padded = pltpu.VMEM((top * PITCH, width), F32)

    def swap(array, turn):
        if turn == 0:
            return array
        return lax.ppermute(array, "ch", [(c, c ^ turn) for c in range(ch_count)])

    message = call(
        functools.partial(forward_kernel, low), "forward", jax.ShapeDtypeStruct((2 * low * PITCH, width), BF16),
        [
            padded,
            pltpu.VMEM((256, 256), BF16),
            pltpu.VMEM((2 * low * PITCH, width), BF16),
            pltpu.SemaphoreType.DMA((4,)),
        ], unit * (low + mid),
        values, factor_low, twist_low.T, factor_mid, twist_top, kernel_low,
        limit=60 << 20, out_spec=pl.BlockSpec(memory_space=pl.ANY),
    )
    message, untwist_t = lax.optimization_barrier((message, untwist_top))
    columns = lax.all_to_all(message.reshape(2 * low, PITCH, width), "seq", 0, 0, tiled=True)

    turns = range(ch_count)
    shares = [lax.dynamic_slice_in_dim(values, (ch_place ^ turn) * share, share, 0) for turn in turns]
    shares = [swap(array, turn) for turn, array in enumerate(shares)]
    weights = [swap(out_weight, turn) for turn in turns]
    silu, matrix = call(
        gate_kernel, "gate",
        [jax.ShapeDtypeStruct((share, columns_out), BF16), jax.ShapeDtypeStruct((ch_count * width, columns_out), BF16)],
        [], unit, *shares, *weights, limit=12 << 20,
    )
    packed = call(
        pack_kernel, "pack", jax.ShapeDtypeStruct(((HALF + 3) * top, width), BF16), [], unit,
        untwist_t, factor_top, inverse_top, inverse_mid, untwist_low.T, limit=8 << 20,
    )
    columns, silu, matrix = lax.optimization_barrier((columns, silu, matrix))
    third = call(
        middle_kernel, "middle", jax.ShapeDtypeStruct((rows, width), BF16),
        [
            pltpu.VMEM((rows, width), BF16),
            padded,
            padded,
            pltpu.VMEM((top, width), F32),
            pltpu.VMEM((HALF, width), F32),
            pltpu.SemaphoreType.DMA((4,)),
        ], unit * (2 * top + mid),
        columns.reshape(top * PITCH, width), kernel_top, packed, limit=24 << 20, out_spec=pl.BlockSpec(memory_space=pltpu.HBM),
    )
    third = lax.all_to_all(third.reshape(top * ch_count, -1, width), ("seq", "ch"), 0, 0, tiled=True)
    return call(
        functools.partial(last_kernel, low), "last", jax.ShapeDtypeStruct((share, columns_out), BF16),
        [
            pltpu.VMEM((share, columns_out), BF16),
            pltpu.VMEM((low * (width + 8), width), F32),
            pltpu.VMEM((share, columns_out), BF16),
            pltpu.VMEM((share, columns_out), BF16),
            pltpu.SemaphoreType.DMA((8,)),
            pltpu.SemaphoreType.DMA((8,)),
        ],
        unit * low // 2 + 2 * share * columns_out ** 2,
        third.reshape(rows, width), inverse_low, silu, matrix,
        limit=24 << 20, far=(2,), out_spec=pl.BlockSpec(memory_space=pl.ANY), aliases={2: 0},
    )


def solution(mesh):
    return jax.shard_map(
        local,
        mesh=mesh,
        in_specs=(
            P("seq", "ch"),
            P(),
            P(),
            P(),
            P(),
            P(),
            P(None, "ch"),
            P("seq", "ch"),
            P(),
            P(),
            P(),
            P(),
            P(),
            P("ch", None),
        ),
        out_specs=P(("seq", "ch"), None),
        check_vma=False,
    )
```

```python
import functools

import jax
import jax.numpy as jnp
from jax import lax
from jax.experimental import pallas as pl
from jax.experimental.pallas import tpu as pltpu
from jax.sharding import PartitionSpec as P

F32 = jnp.float32
BF16 = jnp.bfloat16
LANES = 128
HALF = 64
PITCH = 72


def iota(shape, axis):
    return lax.broadcasted_iota(jnp.int32, shape, axis)


def dot(left, right):
    return jnp.dot(left, right, preferred_element_type=F32)


def repeat_lanes(matrix, times):
    n = matrix.shape[1]
    shape = (n, n * times)
    pick = (lax.rem(iota(shape, 1), n) == iota(shape, 0)).astype(F32).astype(BF16)
    return dot(matrix, pick)


def column_of_row(row):
    n = row.shape[1]
    square = jnp.broadcast_to(row, (n, n))
    return jnp.sum(jnp.where(iota((n, n), 0) == iota((n, n), 1), square, 0.0), axis=1, keepdims=True)


def trade_halves(one, two):
    low = iota(one.shape, 1) < HALF
    return jnp.where(low, one, pltpu.roll(two, HALF, 1)), jnp.where(low, pltpu.roll(one, HALF, 1), two)


def forward_kernel(low, values, factor_low, twist_low, factor_mid, twist_top, kernel_low, message,
                   rows_f, diag, out, sem_out):
    mid = factor_mid.shape[0]
    times = 256 // low
    place = lax.axis_index("seq")
    tiled = repeat_lanes(factor_low[...], times)
    for t in range(times):
        block = jnp.where(iota(tiled.shape, 1) // low == t, tiled, 0.0)
        diag[t * low:(t + 1) * low, :] = block.astype(BF16)
    for n in range(mid * low // 512):
        at = n * 512
        both = dot(diag[...], jnp.concatenate([values[at:at + 256, :], values[at + 256:at + 512, :]], axis=1))
        for t in range(2 * times):
            to = (n * 2 * times + t) * PITCH
            side = t // times * LANES
            at = t % times * low
            rows_f[to:to + low, :] = both[at:at + low, side:side + LANES]
    scaled = column_of_row(twist_top[pl.ds(place, 1), :]) * factor_mid[...].astype(F32)
    profile = kernel_low[...].astype(F32)
    turned = pltpu.roll(profile, HALF, 1)
    stores = []
    for k in range(low):
        matrix = (scaled * twist_low[k:k + 1, :]).astype(BF16)
        second = dot(matrix, rows_f[pl.ds(k, mid, stride=PITCH), :].astype(BF16))
        halves = trade_halves(second[:HALF], second[HALF:])
        for h, (half, line) in enumerate(zip(halves, (profile, turned))):
            to = (2 * k + h) * PITCH
            out[to:to + HALF, :] = half.astype(BF16)
            out[to + HALF:to + PITCH, :] = jnp.broadcast_to(line[k:k + 1, :], (PITCH - HALF, LANES)).astype(BF16)
        if k % 16 == 15:
            size = 32 * PITCH
            at = k // 16 * size
            store = pltpu.make_async_copy(
                out.at[pl.ds(at, size)], message.at[pl.ds(at, size)], sem_out.at[k // 16]
            )
            store.start()
            stores.append(store)
    for store in stores:
        store.wait()


def middle_kernel(columns, packed, spread, third, spread_out,
                  scale, out, rows_f, rows_g, whole, lines, sem_in, sem_out):
    top = packed.shape[1]
    factor_top, inverse_top, inverse_mid = (packed.at[pl.ds(n * top, top)] for n in range(3))
    chunk = HALF // 8 * top
    loads = [
        pltpu.make_async_copy(spread.at[pl.ds(n * chunk, chunk)], scale.at[pl.ds(n * chunk, chunk)], sem_in.at[n])
        for n in range(2)
    ]
    for copy in loads:
        copy.start()
    for n in range(top // 8):
        at = n * 8 * PITCH
        rows_f[at:at + 8 * PITCH, :] = columns[at:at + 8 * PITCH, :].astype(F32)
    rows = rows_f[pl.ds(HALF, 2 * HALF, stride=PITCH), :]
    lines[...] = trade_halves(rows[:HALF], rows[HALF:])[0]
    whole[...] = packed[3 * top:, :].astype(F32)

    def scale_of(r):
        return scale[r // 4 * top:(r // 4 + 1) * top, r % 4 * LANES:(r % 4 + 1) * LANES].astype(F32)

    for r in range(0, HALF, 2):
        if r % 32 == 0:
            loads[r // 32].wait()
        one = rows_f[pl.ds(r, top, stride=PITCH), :].astype(BF16)
        two = rows_f[pl.ds(r + 1, top, stride=PITCH), :].astype(BF16)
        spectrum = dot(factor_top[...], jnp.concatenate([one, two], axis=1)).astype(BF16).astype(F32)
        first = spectrum[:, :LANES] * whole[...] * lines[r:r + 1, :]
        other = spectrum[:, LANES:] * whole[...] * lines[r + 1:r + 2, :]
        filtered = jnp.concatenate([first.astype(BF16), other.astype(BF16)], axis=1)
        back = dot(inverse_top[...], filtered)
        rows_g[pl.ds(r, top, stride=PITCH), :] = back[:, :LANES] * scale_of(r)
        rows_g[pl.ds(r + 1, top, stride=PITCH), :] = back[:, LANES:] * scale_of(r + 1)

    part = 32 * HALF
    stores = []
    for n in range(top // 4):
        sides = []
        for m in range(2):
            at = (n * 4 + m * 2) * PITCH
            upper, under = trade_halves(rows_g[at:at + HALF, :], rows_g[at + PITCH:at + PITCH + HALF, :])
            sides.append(jnp.concatenate([upper.astype(BF16), under.astype(BF16)], axis=0))
        result = dot(inverse_mid[...], jnp.concatenate(sides, axis=1))
        for m in range(2):
            side = result[:, m * LANES:(m + 1) * LANES]
            for q in range(4):
                pair = trade_halves(side[q * 32:q * 32 + 16], side[q * 32 + 16:q * 32 + 32])
                for p in range(2):
                    to = (n * 4 + m * 2 + p) * HALF + q * 16
                    out[to:to + 16, :] = pair[p].astype(BF16)
        if n % 8 == 7:
            at = n // 8 * part
            store = pltpu.make_async_copy(out.at[pl.ds(at, part)], third.at[pl.ds(at, part)], sem_out.at[n // 8])
            store.start()
            stores.append(store)
    for store in stores:
        store.wait()


def pack_kernel(untwist_top, factor_top, inverse_top, inverse_mid, untwist_low, kernel_top, packed, spread):
    top = untwist_top.shape[0]
    place = lax.axis_index("seq")
    shape = (top, LANES)
    lower = iota(shape, 1) < HALF
    for r in range(HALF):
        one = jnp.broadcast_to(untwist_top[:, r:r + 1], shape)
        two = jnp.broadcast_to(untwist_top[:, HALF + r:HALF + r + 1], shape)
        at, side = r // 4 * top, r % 4 * LANES
        spread[at:at + top, side:side + LANES] = jnp.where(lower, one, two).astype(BF16)
    packed[:top, :] = factor_top[...]
    packed[top:2 * top, :] = inverse_top[...]
    column = column_of_row(untwist_low[pl.ds(place // 2, 1), :])
    packed[2 * top:3 * top, :] = (column * inverse_mid[...].astype(F32)).astype(BF16)
    keep = lower == (lax.rem(place, 2) == 0)
    packed[3 * top:, :] = jnp.where(keep, kernel_top[...], pltpu.roll(kernel_top[...], HALF, 1)).astype(BF16)


def gate_kernel(*refs):
    sources, weights, (target, matrix) = refs[:4], refs[4:8], refs[9:]
    for t, (source, weight) in enumerate(zip(sources, weights)):
        matrix[t * LANES:(t + 1) * LANES, :] = weight[...]

        def body(n, _):
            at = pl.multiple_of(n * 256, 256)
            value = source[pl.ds(at, 256), :].astype(F32)
            gate = ((0.5 * value) * (1.0 + jnp.tanh(0.5 * value))).astype(BF16)
            target[pl.ds(at, 256), t * LANES:(t + 1) * LANES] = gate
            return 0

        lax.fori_loop(0, source.shape[0] // 256, body, 0)


def last_kernel(low, third, inverse_low, silu, matrix, out, gates, rows_f, gated, result, sem_in, sem_out):
    pitch = LANES + 8
    block = 4 * low
    place = lax.axis_index("ch")
    fetches = [
        pltpu.make_async_copy(silu.at[pl.ds(at, block)], gates.at[pl.ds(at, block)], sem_in.at[n])
        for n, at in enumerate((p * 4 + g) * block for g in range(4) for p in range(2))
    ]
    for copy in fetches:
        copy.start()
    for k in range(low):
        for h in range(2):
            for t in range(4):
                source = pl.multiple_of(((k * 2 + h) * 4 + (place ^ t)) * 16, 16)
                to = k * pitch + (h * 4 + t) * 16
                rows_f[to:to + 16, :] = third[pl.ds(source, 16), :].astype(F32)
    copies = []
    for copy in fetches:
        copy.wait()
    for g in range(4):
        for b in range(4 * g, 4 * g + 4):
            for t in range(4):
                one = rows_f[pl.ds(t * 16 + b, low, stride=pitch), :]
                two = rows_f[pl.ds((4 + t) * 16 + b, low, stride=pitch), :]
                pair = trade_halves(one, two)
                mixed = dot(inverse_low[...], jnp.concatenate([p.astype(BF16) for p in pair], axis=1))
                for p in range(2):
                    at = (p * 16 + b) * low
                    gated[at:at + low, t * LANES:(t + 1) * LANES] = (
                        mixed[:, p * LANES:(p + 1) * LANES] * gates[at:at + low, t * LANES:(t + 1) * LANES].astype(F32)
                    ).astype(BF16)
        for p in range(2):
            at = (p * 4 + g) * block
            total = dot(gated[at:at + block, :], matrix[...])
            result[at:at + block, :] = total.astype(BF16)
            copy = pltpu.make_async_copy(
                result.at[pl.ds(at, block)], out.at[pl.ds(at, block)], sem_out.at[g * 2 + p]
            )
            copy.start()
            copies.append(copy)
    for copy in copies:
        copy.wait()


def call(kernel, name, out_shape, scratch, flops, *args, limit=40 << 20, far=(), out_spec=None, aliases=None):
    vmem, hbm = pl.BlockSpec(memory_space=pltpu.VMEM), pl.BlockSpec(memory_space=pl.ANY)
    outs = jax.tree.leaves(out_shape)
    moved = sum(a.size * a.dtype.itemsize for a in args) + sum(o.size * o.dtype.itemsize for o in outs)
    return pl.pallas_call(
        kernel,
        name=name,
        out_shape=out_shape,
        in_specs=[hbm if n in far else vmem for n in range(len(args))],
        out_specs=jax.tree.map(lambda _: out_spec or vmem, out_shape),
        scratch_shapes=scratch,
        input_output_aliases=aliases or {},
        compiler_params=pltpu.CompilerParams(vmem_limit_bytes=limit),
        cost_estimate=pl.CostEstimate(flops=flops, bytes_accessed=moved, transcendentals=0),
    )(*args)


def local(
    values,
    factor_low,
    twist_low,
    factor_mid,
    twist_top,
    factor_top,
    kernel_top,
    kernel_low,
    inverse_top,
    untwist_top,
    inverse_mid,
    untwist_low,
    inverse_low,
    out_weight,
):
    low = factor_low.shape[0]
    mid = factor_mid.shape[0]
    top = factor_top.shape[0]
    rows, width = values.shape
    ch_place = lax.axis_index("ch")
    ch_count = lax.axis_size("ch")
    share = rows // ch_count
    columns_out = out_weight.shape[1]
    unit = 2 * rows * width
    padded = pltpu.VMEM((top * PITCH, width), F32)

    def swap(array, turn):
        if turn == 0:
            return array
        return lax.ppermute(array, "ch", [(c, c ^ turn) for c in range(ch_count)])

    message = call(
        functools.partial(forward_kernel, low), "forward", jax.ShapeDtypeStruct((2 * low * PITCH, width), BF16),
        [
            padded,
            pltpu.VMEM((256, 256), BF16),
            pltpu.VMEM((2 * low * PITCH, width), BF16),
            pltpu.SemaphoreType.DMA((4,)),
        ], unit * (low + mid),
        values, factor_low, twist_low.T, factor_mid, twist_top, kernel_low,
        limit=60 << 20, out_spec=pl.BlockSpec(memory_space=pl.ANY),
    )
    message, untwist_t = lax.optimization_barrier((message, untwist_top))
    columns = lax.all_to_all(message.reshape(2 * low, PITCH, width), "seq", 0, 0, tiled=True)

    turns = range(ch_count)
    shares = [lax.dynamic_slice_in_dim(values, (ch_place ^ turn) * share, share, 0) for turn in turns]
    shares = [swap(array, turn) if turn < 3 else array for turn, array in enumerate(shares)]
    result = jax.ShapeDtypeStruct((share, columns_out), BF16)
    packed, spread = call(
        pack_kernel, "pack", [jax.ShapeDtypeStruct((4 * top, width), BF16), result], [], unit,
        untwist_t, factor_top, inverse_top, inverse_mid, untwist_low.T, kernel_top, limit=8 << 20,
    )
    columns, shares = lax.optimization_barrier((columns, shares))
    third, spread = call(
        middle_kernel, "middle", [jax.ShapeDtypeStruct((rows, width), BF16), result],
        [
            pltpu.VMEM((share, columns_out), BF16),
            pltpu.VMEM((rows, width), BF16),
            padded,
            padded,
            pltpu.VMEM((top, width), F32),
            pltpu.VMEM((HALF, width), F32),
            pltpu.SemaphoreType.DMA((2,)),
            pltpu.SemaphoreType.DMA((4,)),
        ], unit * (2 * top + mid),
        columns.reshape(top * PITCH, width), packed, spread,
        limit=24 << 20, far=(2,), aliases={2: 1}, out_spec=pl.BlockSpec(memory_space=pltpu.HBM),
    )
    third, shares, out_weight = lax.optimization_barrier((third, shares, out_weight))
    shares = [swap(array, turn) if turn == 3 else array for turn, array in enumerate(shares)]
    weights = [swap(out_weight, turn) for turn in turns]
    silu, matrix = call(
        gate_kernel, "gate",
        [jax.ShapeDtypeStruct((share, columns_out), BF16), jax.ShapeDtypeStruct((ch_count * width, columns_out), BF16)],
        [], unit, *shares, *weights, spread, limit=12 << 20, far=(8,), aliases={8: 0},
    )
    third = lax.all_to_all(third.reshape(top * ch_count, -1, width), ("seq", "ch"), 0, 0, tiled=True)
    return call(
        functools.partial(last_kernel, low), "last", jax.ShapeDtypeStruct((share, columns_out), BF16),
        [
            pltpu.VMEM((share, columns_out), BF16),
            pltpu.VMEM((low * (width + 8), width), F32),
            pltpu.VMEM((share, columns_out), BF16),
            pltpu.VMEM((share, columns_out), BF16),
            pltpu.SemaphoreType.DMA((8,)),
            pltpu.SemaphoreType.DMA((8,)),
        ],
        unit * low // 2 + 2 * share * columns_out ** 2,
        third.reshape(rows, width), inverse_low, silu, matrix,
        limit=24 << 20, far=(2,), out_spec=pl.BlockSpec(memory_space=pl.ANY), aliases={2: 0},
    )


def solution(mesh):
    return jax.shard_map(
        local,
        mesh=mesh,
        in_specs=(
            P("seq", "ch"),
            P(),
            P(),
            P(),
            P(),
            P(),
            P(None, "ch"),
            P("seq", "ch"),
            P(),
            P(),
            P(),
            P(),
            P(),
            P("ch", None),
        ),
        out_specs=P(("seq", "ch"), None),
        check_vma=False,
    )
```
